32 devices in a mesh: groups: 2 (over y), expert: 4 (over z), seq: 4 (over x, core).
Axes of the slice: x: 2, y: 2, z: 4, core: 2. Of those that a mesh axis runs over, the one named last changes fastest.
Arguments:
- inputs: bfloat16 [4096, 1024], P(('groups', 'expert', 'seq')), parts along dimension 0, may hold values from -6 to 6
- grad_out: bfloat16 [4096, 1024], P(('groups', 'expert', 'seq')), parts along dimension 0, may hold values from -4 to 4
- gates: bfloat16 [4096, 4], P(('groups', 'expert', 'seq')), parts along dimension 0, may hold values from 0.049804688 to 0.59765625
- expert_ids: int32 [4096, 4], P(('groups', 'expert', 'seq')), parts along dimension 0, may hold values from 0 to 3, as said below
- slot_index: int32 [4096, 4], P(('groups', 'expert', 'seq')), parts along dimension 0, may hold values from 0 to 127, as said below
- filter_taps: bfloat16 [256, 1024], replicated, may hold values from -0.375 to 0.375
- w_gate: bfloat16 [4, 1024, 512], P('expert', 'seq'), may hold values from -0.1875 to 0.1875
- w_up: bfloat16 [4, 1024, 512], P('expert', 'seq'), may hold values from -0.1875 to 0.1875
- w_down: bfloat16 [4, 512, 1024], P('expert', 'seq'), may hold values from -0.25 to 0.25
Outputs:
- grad_inputs: bfloat16 [4096, 1024], P(('groups', 'expert', 'seq')), parts along dimension 0
- grad_gates: bfloat16 [4096, 4], P(('groups', 'expert', 'seq')), parts along dimension 0
- grad_filter: float32 [512, 1024], P('groups'), parts along dimension 0
- grad_w_gate: bfloat16 [8, 1024, 512], P(('groups', 'expert'), 'seq'), parts along dimension 0
- grad_w_up: bfloat16 [8, 1024, 512], P(('groups', 'expert'), 'seq'), parts along dimension 0
- grad_w_down: bfloat16 [8, 512, 1024], P(('groups', 'expert'), 'seq'), parts along dimension 0
The draws below stay inside these ranges and needn't reach their ends.
There are 2 independent parts, one for each index of `groups`. The reference program is written for one: setup_inputs(seed, part) draws one part's arguments, and reference() takes and returns one part's arrays. A program takes and returns all parts, laid end to end along the dimension named above; an argument that names none is the same for every part. Nothing has to cross between parts.
Inputs may be any that keep to these rules, and one draw needn't show every extreme that they name: `expert_ids`: each row names 4 different experts, and every expert is named by some row. Among the assignments of the 128 rows of one device that name the same expert, slot_index takes each of the values 0, 1, ... once, in an order of priority that is not row order; assignments with a slot of 128 or more are dropped.
All inputs are finite; a program needn't handle non-finite values.
Results may differ from the reference program's by a relative error of at most 0.009.
Values may be sent and summed in bfloat16 or wider, within the bound.
A program may use at most 64 MiB of HBM per device.

```python
import jax
import jax.numpy as jnp
from jax import lax

D = 1024
FF = 512
TAPS = 256
TOP = 4
TOK_DEV = 128
SPECIALIST_COUNT = 4
CAP = 128
LENGTH = 512
TOKENS = 2048
N_EXPERT = 4
N_SEQ = 4


def device_ranks(item):
    chosen_flat, priority = item
    same = chosen_flat[:, None] == chosen_flat[None, :]
    before = priority[None, :] < priority[:, None]
    return jnp.sum((same & before).astype(jnp.int32), axis=1).astype(jnp.int32)


def routing(key):
    drawn_router_preference = jax.random.fold_in(key, 7)
    busiest_rng_branch, favour_rng_branch, jitter_rng_branch = jax.random.split(drawn_router_preference, 3)
    priority_branch = jax.random.fold_in(key, 11)
    busiest_specialist = jax.random.randint(busiest_rng_branch, (), 0, SPECIALIST_COUNT)
    lane_positions = jnp.arange(SPECIALIST_COUNT, dtype=jnp.int32)
    extra_favour_amount = jax.random.randint(favour_rng_branch, (SPECIALIST_COUNT,), 0, 2 ** 20)
    extra_favour_amount = jnp.where(lane_positions == busiest_specialist, 2 ** 21, extra_favour_amount)
    position_mod = jnp.arange(TOKENS, dtype=jnp.int32) % SPECIALIST_COUNT
    pinned_specialist = jnp.where(lane_positions[None, :] == position_mod[:, None], 2 ** 21 - 1, 0)
    jitter_draw = jax.random.randint(jitter_rng_branch, (TOKENS, SPECIALIST_COUNT), 0, 2 ** 20)
    dispatch_preference = (jitter_draw + jnp.maximum(extra_favour_amount[None, :], pinned_specialist)) * SPECIALIST_COUNT + lane_positions[None, :]
    chosen = lax.top_k(dispatch_preference, TOP)[1].astype(jnp.int32)
    blocks = TOKENS // TOK_DEV
    per_block = TOK_DEV * TOP
    local_index = jnp.arange(per_block, dtype=jnp.int32)
    high_part = jax.random.randint(priority_branch, (blocks, per_block), 0, 2 ** 12)
    priority = high_part * per_block + local_index[None, :]
    placed = lax.map(device_ranks, (chosen.reshape(blocks, per_block), priority))
    return (chosen, placed.reshape(TOKENS, TOP).astype(jnp.int32))


def draw_expert_ids(key, part):
    return routing(key)[0]


def draw_slot_index(key, part):
    return routing(key)[1]


def shard_levels(key, extent, cuts, least, top_value):
    factor_of = 1.0
    for dim, blocks in cuts:
        steps = jax.random.uniform(jax.random.fold_in(jax.random.fold_in(key, 6), dim), (blocks,), jnp.float32, least / len(cuts), top_value / len(cuts))
        factor_of = factor_of * jnp.repeat(jnp.exp(steps), extent[dim] // blocks).reshape((-1,) + (1,) * (len(extent) - 1 - dim))
    return factor_of


def gaussian(stream_key, shape, width, most, cuts=(), kind=jnp.bfloat16):
    factor_of = shard_levels(stream_key, shape, cuts, -0.22, 0.18) if cuts else 1.0
    entries = jax.random.normal(stream_key, shape, jnp.float32) * width * factor_of
    return jnp.minimum(jnp.maximum(entries, -most), most).astype(kind)


def setup_inputs(seed: int = 0, part: int = 0) -> dict:
    key_list = jax.random.split(jax.random.key(seed), 10)
    own_keys = jax.random.split(jax.random.fold_in(key_list[9], part), 10)
    inputs = gaussian(own_keys[0], (TOKENS, D), 1.0, 6.0, ((0, 16),))
    grad_out = gaussian(own_keys[1], (TOKENS, D), 0.25, 4.0, ((0, 16),))
    gates = jnp.clip(0.049804688 + 0.54785156 * jax.random.uniform(own_keys[2], (TOKENS, TOP), jnp.float32) ** shard_levels(own_keys[2], (TOKENS, TOP), ((0, 16),), -0.2, 0.2), 0.049804688, 0.59765625).astype(jnp.bfloat16)
    expert_ids = draw_expert_ids(jax.random.fold_in(jax.random.fold_in(key_list[9], part), 71), part)
    slot_index = draw_slot_index(jax.random.fold_in(jax.random.fold_in(key_list[9], part), 71), part)
    filter_taps = gaussian(key_list[5], (TAPS, D), TAPS ** -0.5, 0.375)
    w_gate = gaussian(key_list[6], (SPECIALIST_COUNT, D, FF), D ** -0.5, 0.1875, ((0, 4), (1, 4)))
    w_up = gaussian(key_list[7], (SPECIALIST_COUNT, D, FF), D ** -0.5, 0.1875, ((0, 4), (1, 4)))
    w_down = gaussian(key_list[8], (SPECIALIST_COUNT, FF, D), FF ** -0.5, 0.25, ((0, 4), (1, 4)))
    return dict(inputs=inputs, grad_out=grad_out, gates=gates, expert_ids=expert_ids, slot_index=slot_index, filter_taps=filter_taps, w_gate=w_gate, w_up=w_up, w_down=w_down)


def contract(left, right, left_dim, right_dim):
    return lax.dot_general(left, right, (((left_dim,), (right_dim,)), ((), ())), preferred_element_type=jnp.float32)

def causal_filter(padded, taps_f):

    def add_tap(tap, total):
        window = lax.dynamic_slice_in_dim(padded, TAPS - 1 - tap, LENGTH, 1)
        weights = lax.dynamic_slice_in_dim(taps_f, tap, 1, 0)
        return total + weights[None] * window
    return lax.fori_loop(0, TAPS, add_tap, jnp.zeros((N_EXPERT, LENGTH, D), jnp.float32))

def anticausal_filter(grad_padded, taps_f):

    def add_tap(tap, total):
        window = lax.dynamic_slice_in_dim(grad_padded, tap, LENGTH, 1)
        weights = lax.dynamic_slice_in_dim(taps_f, tap, 1, 0)
        return total + weights[None] * window
    return lax.fori_loop(0, TAPS, add_tap, jnp.zeros((N_EXPERT, LENGTH, D), jnp.float32))

def expert_block(item):
    token_buf, scaled_buf, gate_mat, up_mat, down_mat = item
    grad_list = []
    output_list = []
    sum_gate = jnp.zeros(gate_mat.shape, jnp.float32)
    sum_up = jnp.zeros(up_mat.shape, jnp.float32)
    sum_down = jnp.zeros(down_mat.shape, jnp.float32)
    for quarter in range(N_SEQ):
        token_rows = token_buf[quarter]
        scaled_rows = scaled_buf[quarter]
        pre_gate = jnp.dot(token_rows, gate_mat, preferred_element_type=jnp.float32)
        pre_up = jnp.dot(token_rows, up_mat, preferred_element_type=jnp.float32)
        sigma = jax.nn.sigmoid(pre_gate)
        swish = pre_gate * sigma
        hidden = (swish * pre_up).astype(jnp.bfloat16)
        output_list.append(jnp.dot(hidden, down_mat, preferred_element_type=jnp.float32).astype(jnp.bfloat16))
        grad_hidden = contract(scaled_rows, down_mat, 1, 1)
        grad_pre_gate = (grad_hidden * pre_up * (sigma * (1.0 + pre_gate * (1.0 - sigma)))).astype(jnp.bfloat16)
        grad_pre_up = (grad_hidden * swish).astype(jnp.bfloat16)
        part_gate = lax.optimization_barrier(contract(token_rows, grad_pre_gate, 0, 0).astype(jnp.bfloat16))
        part_up = lax.optimization_barrier(contract(token_rows, grad_pre_up, 0, 0).astype(jnp.bfloat16))
        part_down = lax.optimization_barrier(contract(hidden, scaled_rows, 0, 0).astype(jnp.bfloat16))
        sum_gate = sum_gate + part_gate.astype(jnp.float32)
        sum_up = sum_up + part_up.astype(jnp.float32)
        sum_down = sum_down + part_down.astype(jnp.float32)
        grad_rows = contract(grad_pre_gate, gate_mat, 1, 1) + contract(grad_pre_up, up_mat, 1, 1)
        grad_list.append(grad_rows.astype(jnp.bfloat16))
    return (jnp.stack(grad_list), jnp.stack(output_list), sum_gate.astype(jnp.bfloat16), sum_up.astype(jnp.bfloat16), sum_down.astype(jnp.bfloat16))

def reference(inputs, grad_out, gates, expert_ids, slot_index, filter_taps, w_gate, w_up, w_down):
    taps_f = filter_taps.astype(jnp.float32)
    seq_inputs = inputs.astype(jnp.float32).reshape(N_EXPERT, LENGTH, D)
    padded = jnp.pad(seq_inputs, ((0, 0), (TAPS - 1, 0), (0, 0)))
    filtered = causal_filter(padded, taps_f).reshape(TOKENS, D).astype(jnp.bfloat16)
    kept = slot_index < CAP
    device = jnp.arange(TOKENS, dtype=jnp.int32) // TOK_DEV
    source = (device // N_SEQ)[:, None]
    quarter = (device % N_SEQ)[:, None]
    limit = SPECIALIST_COUNT * N_SEQ * N_EXPERT * CAP
    dest = jnp.where(kept, ((expert_ids * N_SEQ + quarter) * N_EXPERT + source) * CAP + slot_index, limit)
    dest = dest.reshape(-1).astype(jnp.int32)
    token_rows = jnp.broadcast_to(filtered[:, None, :], (TOKENS, TOP, D)).reshape(-1, D)
    scaled = (gates.astype(jnp.float32)[:, :, None] * grad_out.astype(jnp.float32)[:, None, :]).astype(jnp.bfloat16).reshape(-1, D)
    block_rows = N_EXPERT * CAP
    token_buf = jnp.zeros((limit, D), jnp.bfloat16).at[dest].set(token_rows, mode='drop').reshape(SPECIALIST_COUNT, N_SEQ, block_rows, D)
    scaled_buf = jnp.zeros((limit, D), jnp.bfloat16).at[dest].set(scaled, mode='drop').reshape(SPECIALIST_COUNT, N_SEQ, block_rows, D)
    grad_buf, output_buf, grad_w_gate, grad_w_up, grad_w_down = lax.map(expert_block, (token_buf, scaled_buf, w_gate, w_up, w_down))
    grad_back = jnp.take(grad_buf.reshape(limit, D), dest, axis=0, mode='fill', fill_value=0).reshape(TOKENS, TOP, D)
    output_back = jnp.take(output_buf.reshape(limit, D), dest, axis=0, mode='fill', fill_value=0).reshape(TOKENS, TOP, D)
    grad_gates = lax.optimization_barrier(jnp.sum(grad_out.astype(jnp.float32)[:, None, :] * output_back.astype(jnp.float32), axis=2)).astype(jnp.bfloat16)
    grad_filtered = lax.optimization_barrier(jnp.sum(grad_back.astype(jnp.float32), axis=1)).astype(jnp.bfloat16)
    seq_grad = grad_filtered.astype(jnp.float32).reshape(N_EXPERT, LENGTH, D)
    grad_padded = jnp.pad(seq_grad, ((0, 0), (0, TAPS - 1), (0, 0)))
    grad_inputs = anticausal_filter(grad_padded, taps_f).reshape(TOKENS, D).astype(jnp.bfloat16)

    def tap_grad(tap):
        window = lax.dynamic_slice_in_dim(padded, TAPS - 1 - tap, LENGTH, 1)
        return lax.optimization_barrier(jnp.sum(seq_grad * window, axis=(0, 1)))
    grad_filter = lax.map(tap_grad, jnp.arange(TAPS, dtype=jnp.int32))
    return (grad_inputs, grad_gates, grad_filter, grad_w_gate, grad_w_up, grad_w_down)
```

```python
import functools

import jax
import jax.numpy as jnp
import numpy as np
from jax import lax
from jax.experimental import pallas as pl
from jax.experimental.pallas import tpu as pltpu
from jax.sharding import PartitionSpec as P

MESH = pl.DeviceIdType.MESH
F32 = jnp.float32
BF16 = jnp.bfloat16


def from_behind(block, axis, distance):
    devices = range(lax.axis_size(axis))
    route = [(i - distance, i) for i in devices if i - distance in devices]
    return lax.ppermute(block, axis, route)


def depthwise(signal, kernel):
    return lax.conv_general_dilated(
        signal[None],
        kernel[:, None, :],
        (1,),
        "VALID",
        dimension_numbers=("NWC", "WIO", "NWC"),
        feature_group_count=signal.shape[1],
        preferred_element_type=jnp.float32,
    )[0]


def contract(left, right, left_dim, right_dim):
    return lax.dot_general(
        left, right, (((left_dim,), (right_dim,)), ((), ())), preferred_element_type=jnp.float32
    )


def expert_pass(token_rows, scaled_rows, gate_mat, up_mat, down_mat):
    pre_gate = jnp.dot(token_rows, gate_mat, preferred_element_type=jnp.float32)
    pre_up = jnp.dot(token_rows, up_mat, preferred_element_type=jnp.float32)
    sigma = jax.nn.sigmoid(pre_gate)
    swish = pre_gate * sigma
    hidden = (swish * pre_up).astype(jnp.bfloat16)
    outputs = jnp.dot(hidden, down_mat, preferred_element_type=jnp.float32).astype(jnp.bfloat16)
    grad_hidden = contract(scaled_rows, down_mat, 1, 1)
    grad_pre_gate = (grad_hidden * pre_up * (sigma * (1.0 + pre_gate * (1.0 - sigma)))).astype(
        jnp.bfloat16
    )
    grad_pre_up = (grad_hidden * swish).astype(jnp.bfloat16)
    part_gate = contract(token_rows, grad_pre_gate, 0, 0)
    part_up = contract(token_rows, grad_pre_up, 0, 0)
    part_down = contract(hidden, scaled_rows, 0, 0)
    grad_rows = (
        contract(grad_pre_gate, gate_mat, 1, 1) + contract(grad_pre_up, up_mat, 1, 1)
    ).astype(jnp.bfloat16)
    return (grad_rows, outputs, (part_gate, part_up, part_down))


def routed_body(inputs, grad_out, gates, expert_ids, slot_index, filter_taps, w_gate, w_up, w_down):
    tok_count, width = inputs.shape
    taps = filter_taps.shape[0]
    top_count = expert_ids.shape[1]
    experts = lax.axis_size("expert")
    capacity = tok_count * top_count // experts
    reach = taps - 1
    shift_count = (reach + tok_count - 1) // tok_count
    earlier = [from_behind(inputs, "seq", shift_by) for shift_by in range(shift_count, 0, -1)]
    extended = jnp.concatenate(earlier + [inputs], axis=0)[-(tok_count + reach) :]
    filtered = depthwise(extended, filter_taps[::-1]).astype(jnp.bfloat16)
    kept = slot_index < capacity
    dest = jnp.where(kept, expert_ids * capacity + slot_index, experts * capacity).reshape(-1)

    def place(values):
        rest = values.shape[1:]
        empty = jnp.zeros((experts * capacity,) + rest, values.dtype)
        return empty.at[dest].set(values, mode="drop").reshape((experts, capacity) + rest)

    def fetch(buffer):
        rest = buffer.shape[2:]
        flat = buffer.reshape((experts * capacity,) + rest)
        return jnp.take(flat, dest, axis=0, mode="fill", fill_value=0).reshape(
            (tok_count, top_count) + rest
        )

    token_send = place(
        jnp.broadcast_to(filtered[:, None, :], (tok_count, top_count, width)).reshape(-1, width)
    )
    gate_full, up_full, down_full = (
        lax.all_gather(w_gate, "seq", axis=1, tiled=True),
        lax.all_gather(w_up, "seq", axis=1, tiled=True),
        lax.all_gather(w_down, "seq", axis=1, tiled=True),
    )
    gate_mat = gate_full[0]
    up_mat = up_full[0]
    down_mat = down_full[0]
    scaled = (
        gates.astype(jnp.float32)[:, :, None] * grad_out.astype(jnp.float32)[:, None, :]
    ).astype(jnp.bfloat16)
    token_recv, scaled_recv = (
        lax.all_to_all(token_send, "expert", split_axis=0, concat_axis=0, tiled=True),
        lax.all_to_all(
            place(scaled.reshape(-1, width)), "expert", split_axis=0, concat_axis=0, tiled=True
        ),
    )
    grad_rows, outputs, partials = expert_pass(
        token_recv.reshape(-1, width), scaled_recv.reshape(-1, width), gate_mat, up_mat, down_mat
    )
    grad_back, output_back = (
        lax.all_to_all(
            grad_rows.reshape(experts, capacity, width),
            "expert",
            split_axis=0,
            concat_axis=0,
            tiled=True,
        ),
        lax.all_to_all(
            outputs.reshape(experts, capacity, width),
            "expert",
            split_axis=0,
            concat_axis=0,
            tiled=True,
        ),
    )
    output_rows = fetch(output_back)
    grad_gates = jnp.sum(
        grad_out.astype(jnp.float32)[:, None, :] * output_rows.astype(jnp.float32), axis=2
    ).astype(jnp.bfloat16)
    summed_gate, summed_up, summed_down = (
        lax.psum_scatter(
            partials[0][None].astype(jnp.bfloat16), "seq", scatter_dimension=1, tiled=True
        ).astype(jnp.float32),
        lax.psum_scatter(
            partials[1][None].astype(jnp.bfloat16), "seq", scatter_dimension=1, tiled=True
        ).astype(jnp.float32),
        lax.psum_scatter(
            partials[2][None].astype(jnp.bfloat16), "seq", scatter_dimension=1, tiled=True
        ).astype(jnp.float32),
    )
    grad_filtered = jnp.sum(fetch(grad_back).astype(jnp.float32), axis=1).astype(jnp.bfloat16)
    later = [from_behind(grad_filtered, "seq", -shift_by) for shift_by in range(1, shift_count + 1)]
    grad_extended = jnp.concatenate([grad_filtered] + later, axis=0)[: tok_count + reach]
    grad_inputs = depthwise(grad_extended, filter_taps).astype(jnp.bfloat16)
    local_taps = depthwise(extended, grad_filtered)[::-1]
    grad_filter = lax.psum(local_taps, ("expert", "seq"))
    return (
        grad_inputs,
        grad_gates,
        grad_filter,
        summed_gate.astype(jnp.bfloat16),
        summed_up.astype(jnp.bfloat16),
        summed_down.astype(jnp.bfloat16),
    )


def transforms(size):
    freq = 2.0 * np.pi * (np.arange(size // 2) + 0.5) / size
    angle = freq[:, None] * np.arange(size)[None, :]
    forward = np.concatenate([np.cos(angle), np.sin(angle)], axis=0)
    inverse = forward.T * (2.0 / size)

    def pieces(matrix):
        high = matrix.astype(jnp.bfloat16)
        low = (matrix - high.astype(np.float64)).astype(jnp.bfloat16)
        return high, low

    return pieces(forward) + pieces(inverse)


def mm(left, right):
    return jnp.dot(left, right, preferred_element_type=F32)


def dense_kernel(
    rows_ref, cot_ref, pack_ref, taps_ref, fh_ref, fl_ref, ih_ref, il_ref,
    gin_ref, gg_ref, gf_ref, gw_ref,
    xext, tap_spec, x_spec, tall, gall, wall, hid, gpre, scaled, back, rall,
    part, sib_in, pair, cross_in, gext, gfs, gf_in, gfz, gfz_in, gfo, gfull,
    send_sem, recv_sem,
):
    z = lax.axis_index("expert")
    q = lax.axis_index("seq")
    tok, width = rows_ref.shape
    size = xext.shape[0]
    half = size // 2
    reach_at = size - tok
    dq = 2 * tok
    ff = hid.shape[1]
    fq = ff // 4
    chunk = 256
    chunks = width // chunk
    sib = q + 1 - 2 * (q % 2)
    cross = (q + 2) % 4
    far = (sib + 2) % 4

    def link(n, src, dst, axis, peer):
        return pltpu.make_async_remote_copy(
            src_ref=src, dst_ref=dst, send_sem=send_sem.at[n], recv_sem=recv_sem.at[n],
            device_id={axis: peer}, device_id_type=MESH,
        )

    barrier = pltpu.get_barrier_semaphore()
    for s in range(1, 4):
        pl.semaphore_signal(barrier, inc=1, device_id={"expert": (z + s) % 4}, device_id_type=MESH)
        pl.semaphore_signal(barrier, inc=1, device_id={"seq": (q + s) % 4}, device_id_type=MESH)
    pl.semaphore_wait(barrier, 6)

    halo = [
        link(n, rows_ref, xext.at[pl.ds(reach_at - (n + 1) * tok, tok)], "seq", (q + n + 1) % 4)
        for n in range(2)
    ]
    for n in range(2):
        @pl.when(q + n + 1 < 4)
        def _(n=n):
            halo[n].start()

        @pl.when(q < n + 1)
        def _(n=n):
            xext[pl.ds(reach_at - (n + 1) * tok, tok)] = jnp.zeros((tok, width), BF16)

    cots = [link(1 + s, cot_ref, gall.at[s], "expert", (z + s) % 4) for s in range(1, 4)]
    for copy in cots:
        copy.start()
    w_sib = link(8, pack_ref, wall.at[q], "seq", sib)
    w_cross = link(9, pack_ref, wall.at[q], "seq", cross)
    w_sib.start()
    w_cross.start()
    wall[q] = pack_ref[...]
    gall[0] = cot_ref[...]
    xext[pl.ds(reach_at, tok)] = rows_ref[...]

    def cols(c):
        return pl.ds(pl.multiple_of(c * chunk, chunk), chunk)

    def forward(first, count, values):
        span = slice(first, first + count)
        return mm(fh_ref[:, span], values) + mm(fl_ref[:, span], values)

    def backward(first, count, spec):
        span = slice(first, first + count)
        high = spec.astype(BF16)
        low = (spec - high.astype(F32)).astype(BF16)
        return mm(ih_ref[span], high) + mm(il_ref[span], high) + mm(ih_ref[span], low)

    taps = taps_ref.shape[0]

    @pl.loop(0, chunks)
    def _(c):
        tap_spec[:, cols(c)] = forward(0, taps, taps_ref[:, cols(c)])

    for n in range(2):
        @pl.when(q >= n + 1)
        def _(n=n):
            halo[n].wait_recv()

    @pl.loop(0, chunks)
    def _(c):
        spec = forward(0, size, xext[:, cols(c)])
        x_spec[:, cols(c)] = spec
        xc, xs = spec[:half], spec[half:]
        hc, hs = tap_spec[:half, cols(c)], tap_spec[half:, cols(c)]
        prod = jnp.concatenate([xc * hc - xs * hs, xc * hs + xs * hc], axis=0)
        tall[0, :, cols(c)] = backward(reach_at, tok, prod).astype(BF16)

    rows_out = [link(4 + s, tall.at[0], tall.at[s], "expert", (z + s) % 4) for s in range(1, 4)]
    for copy in rows_out:
        copy.start()

    w_cross.wait_recv()
    w_far = link(10, wall.at[cross], wall.at[cross], "seq", sib)
    w_far.start()
    w_sib.wait_recv()
    w_far.wait_recv()

    def turned(left, right):
        return lax.dot_general(left, right, (((1,), (1,)), ((), ())), preferred_element_type=F32)

    lanes = lax.broadcasted_iota(jnp.int32, (tok, 128), 1)
    backs = [
        link(10 + s, back.at[s], rall.at[s], "expert", (z + 4 - s) % 4) for s in range(1, 4)
    ]
    for s in range(4):
        if s:
            cots[s - 1].wait_recv()
            rows_out[s - 1].wait_recv()
        span = pl.ds(s * tok, tok)
        pre = mm(tall[s, :, 0:dq], wall[0, :dq, :])
        for k in range(1, 4):
            pre += mm(tall[s, :, k * dq:(k + 1) * dq], wall[k, :dq, :])
        cot = gall[s, :, :width]
        weight = jnp.sum(
            jnp.where(lanes == z, gall[s, :, width:].astype(F32), 0.0), axis=1, keepdims=True
        )
        raw = jnp.concatenate([turned(cot, wall[k, dq:, :]) for k in range(4)], axis=1)
        gate, up = pre[:, :ff], pre[:, ff:]
        sigma = jax.nn.sigmoid(gate)
        swish = gate * sigma
        hidden = (swish * up).astype(BF16)
        gg = jnp.sum(hidden.astype(F32) * raw, axis=1, keepdims=True)
        grad_hidden = raw * weight
        grad_gate = grad_hidden * up * (sigma * (1.0 + gate * (1.0 - sigma)))
        gp = jnp.concatenate([grad_gate.astype(BF16), (grad_hidden * swish).astype(BF16)], axis=1)
        hid[span] = hidden
        gpre[span] = gp
        scaled[span] = (weight * cot.astype(F32)).astype(BF16)
        target = back if s else rall
        for k in range(4):
            target[s, :, k * dq:(k + 1) * dq] = turned(gp, wall[k, :dq, :]).astype(BF16)
        target[s, :, width:] = jnp.broadcast_to(gg, (tok, 128)).astype(BF16)
        if s:
            backs[s - 1].start()

    def across(left, right):
        return lax.dot_general(left, right, (((0,), (0,)), ((), ())), preferred_element_type=F32)

    def partial(slot, dest):
        top = jnp.zeros((dq, 2 * ff), F32)
        low = jnp.zeros((fq, width), F32)
        wide = pl.ds(pl.multiple_of(dest * dq, dq), dq)
        thin = pl.ds(pl.multiple_of(dest * fq, fq), fq)
        for s in range(4):
            top += across(tall[s, :, wide], gpre[pl.ds(s * tok, tok)])
        low = across(hid[:, thin], scaled[...])
        part[slot, :dq] = top.astype(BF16)
        part[slot, dq:] = low.astype(BF16)

    to_sib = [link(14 + n, part.at[n], sib_in.at[n], "seq", sib) for n in range(2)]
    partial(0, far)
    to_sib[0].start()
    partial(1, sib)
    to_sib[1].start()
    partial(2, cross)

    for copy in backs:
        copy.wait_recv()
    total = jnp.zeros((tok, width), F32)
    gates_all = jnp.zeros((tok, 128), F32)
    for s in range(4):
        total += rall[s, :, :width].astype(F32)
        gates_all += jnp.where(lanes == (z + s) % 4, rall[s, :, width:].astype(F32), 0.0)
    gg_ref[...] = gates_all
    gext[pl.ds(0, tok)] = total.astype(BF16)
    halo_back = [
        link(17 + n, gext.at[pl.ds(0, tok)], gext.at[pl.ds((n + 1) * tok, tok)], "seq", (q + 3 - n) % 4)
        for n in range(2)
    ]
    for n in range(2):
        @pl.when(q >= n + 1)
        def _(n=n):
            halo_back[n].start()

        @pl.when(q + n + 1 >= 4)
        def _(n=n):
            gext[pl.ds((n + 1) * tok, tok)] = jnp.zeros((tok, width), BF16)

    to_sib[0].wait_recv()
    pair[...] = (part[2].astype(F32) + sib_in[0].astype(F32)).astype(BF16)
    to_cross = link(16, pair, cross_in, "seq", cross)

    quarter = taps // 4

    @pl.loop(0, chunks)
    def _(c):
        spec = forward(reach_at, tok, gext[pl.ds(0, tok), cols(c)])
        gc, gs = spec[:half], spec[half:]
        xc, xs = x_spec[:half, cols(c)], x_spec[half:, cols(c)]
        prod = jnp.concatenate([gc * xc + gs * xs, gs * xc - gc * xs], axis=0)
        result = backward(0, taps, prod).astype(BF16)
        for k in range(4):
            gfs[k, :, cols(c)] = result[k * quarter:(k + 1) * quarter]

    gf_seq = [
        link(18 + s, gfs.at[(q + s) % 4], gf_in.at[s], "seq", (q + s) % 4) for s in range(1, 4)
    ]
    for copy in gf_seq:
        copy.start()
    to_cross.start()
    partial(3, q)

    for copy in gf_seq:
        copy.wait_recv()
    mine = gfs[q].astype(F32)
    for s in range(1, 4):
        mine += gf_in[s].astype(F32)
    piece = quarter // 4
    for k in range(4):
        gfz[k] = mine[k * piece:(k + 1) * piece].astype(BF16)
    gf_exp = [
        link(21 + s, gfz.at[(z + s) % 4], gfz_in.at[s], "expert", (z + s) % 4) for s in range(1, 4)
    ]
    for copy in gf_exp:
        copy.start()

    for n in range(2):
        @pl.when(q + n + 1 < 4)
        def _(n=n):
            halo_back[n].wait_recv()

    for copy in gf_exp:
        copy.wait_recv()
    mine = gfz[z].astype(F32)
    for s in range(1, 4):
        mine += gfz_in[s].astype(F32)
    gfull[q, z] = mine.astype(BF16)
    gf_out = [
        link(24 + s, gfull.at[q, z], gfull.at[q, z], "expert", (z + s) % 4) for s in range(1, 4)
    ]
    for copy in gf_out:
        copy.start()

    @pl.loop(0, chunks)
    def _(c):
        spec = forward(0, size, gext[:, cols(c)])
        gc, gs = spec[:half], spec[half:]
        hc, hs = tap_spec[:half, cols(c)], tap_spec[half:, cols(c)]
        prod = jnp.concatenate([gc * hc + gs * hs, gs * hc - gc * hs], axis=0)
        gin_ref[:, cols(c)] = backward(0, tok, prod).astype(BF16)

    for copy in gf_out:
        copy.wait_recv()
    gf_last = [link(27 + s, gfull.at[q], gfull.at[q], "seq", (q + s) % 4) for s in range(1, 4)]
    for copy in gf_last:
        copy.start()

    to_sib[1].wait_recv()
    to_cross.wait_recv()
    gw_ref[...] = (
        part[3].astype(F32) + sib_in[1].astype(F32) + cross_in[...].astype(F32)
    ).astype(BF16)

    for copy in gf_last:
        copy.wait_recv()
    for a in range(4):
        for b in range(4):
            gf_ref[pl.ds((a * 4 + b) * piece, piece)] = gfull[a, b].astype(F32)

    for n in range(2):
        @pl.when(q + n + 1 < 4)
        def _(n=n):
            halo[n].wait_send()

        @pl.when(q >= n + 1)
        def _(n=n):
            halo_back[n].wait_send()
    for copy in (
        cots + [w_sib, w_cross, w_far] + rows_out + backs + to_sib + [to_cross]
        + gf_seq + gf_exp + gf_out + gf_last
    ):
        copy.wait_send()


def dense_body(inputs, grad_out, gates, expert_ids, slot_index, filter_taps, w_gate, w_up, w_down):
    tok, width = inputs.shape
    taps = filter_taps.shape[0]
    ff = w_gate.shape[2]
    experts = expert_ids.shape[1]
    size = taps + tok
    kept = slot_index < tok
    named = (expert_ids[:, :, None] == jnp.arange(experts)[None, None, :]) & kept[:, :, None]
    by_expert = jnp.sum(jnp.where(named, gates.astype(F32)[:, :, None], 0.0), axis=1).astype(BF16)
    cot = jnp.concatenate([grad_out, jnp.pad(by_expert, ((0, 0), (0, 128 - experts)))], axis=1)
    pack = jnp.concatenate([jnp.concatenate([w_gate[0], w_up[0]], axis=1), w_down[0]], axis=0)
    rows = pack.shape[0]
    ext = width + 128
    vm = lambda *shape: pltpu.VMEM(shape, BF16)
    grad_inputs, gate_grads, grad_filter, weights = pl.pallas_call(
        dense_kernel,
        out_shape=(
            jax.ShapeDtypeStruct((tok, width), BF16),
            jax.ShapeDtypeStruct((tok, 128), F32),
            jax.ShapeDtypeStruct((taps, width), F32),
            jax.ShapeDtypeStruct((rows, width), BF16),
        ),
        in_specs=[pl.BlockSpec(memory_space=pltpu.VMEM)] * 8,
        out_specs=(pl.BlockSpec(memory_space=pltpu.VMEM),) * 4,
        scratch_shapes=[
            vm(size, width), pltpu.VMEM((size, width), F32), pltpu.VMEM((size, width), F32),
            vm(4, tok, width), vm(4, tok, ext), vm(4, rows, width),
            vm(4 * tok, ff), vm(4 * tok, 2 * ff), vm(4 * tok, width),
            vm(4, tok, ext), vm(4, tok, ext),
            vm(4, rows, width), vm(2, rows, width), vm(rows, width), vm(rows, width),
            vm(size, width), vm(4, taps // 4, width), vm(4, taps // 4, width),
            vm(4, taps // 16, width), vm(4, taps // 16, width), vm(8, 128),
            vm(4, 4, taps // 16, width),
            pltpu.SemaphoreType.DMA((32,)), pltpu.SemaphoreType.DMA((32,)),
        ],
        compiler_params=pltpu.CompilerParams(
            collective_id=0, has_side_effects=True, vmem_limit_bytes=52 * 1024 * 1024
        ),
    )(inputs, cot, pack, filter_taps, *[jnp.asarray(m) for m in transforms(size)])
    picked = jnp.where(named, gate_grads[:, None, :experts], 0.0)
    grad_gates = jnp.sum(picked, axis=2).astype(BF16)
    dq = w_gate.shape[1]
    return (
        grad_inputs,
        grad_gates,
        grad_filter,
        weights[None, :dq, :ff],
        weights[None, :dq, ff:],
        weights[None, dq:, :],
    )


def body_of(mesh):
    def body(*args):
        top_count = args[3].shape[1]
        tok, taps, dq = args[0].shape[0], args[5].shape[0], args[6].shape[1]
        small = mesh.shape["expert"] == top_count == 4 and mesh.shape["seq"] == 4
        if small and taps == 2 * tok and dq == 2 * tok and 2 * args[6].shape[2] == args[0].shape[1]:
            return dense_body(*args)
        return routed_body(*args)

    return body


def solution(mesh):
    return jax.shard_map(
        body_of(mesh),
        mesh=mesh,
        in_specs=(
            P(("groups", "expert", "seq"), None),
            P(("groups", "expert", "seq"), None),
            P(("groups", "expert", "seq"), None),
            P(("groups", "expert", "seq"), None),
            P(("groups", "expert", "seq"), None),
            P(),
            P("expert", "seq", None),
            P("expert", "seq", None),
            P("expert", "seq", None),
        ),
        out_specs=(
            P(("groups", "expert", "seq"), None),
            P(("groups", "expert", "seq"), None),
            P("groups", None),
            P(("groups", "expert"), "seq", None),
            P(("groups", "expert"), "seq", None),
            P(("groups", "expert"), "seq", None),
        ),
        check_vma=False,
    )
```

```python
import functools

import jax
import jax.numpy as jnp
import numpy as np
from jax import lax
from jax.experimental import pallas as pl
from jax.experimental.pallas import tpu as pltpu
from jax.sharding import PartitionSpec as P

MESH = pl.DeviceIdType.MESH
F32 = jnp.float32
BF16 = jnp.bfloat16


def from_behind(block, axis, distance):
    devices = range(lax.axis_size(axis))
    route = [(i - distance, i) for i in devices if i - distance in devices]
    return lax.ppermute(block, axis, route)


def depthwise(signal, kernel):
    return lax.conv_general_dilated(
        signal[None],
        kernel[:, None, :],
        (1,),
        "VALID",
        dimension_numbers=("NWC", "WIO", "NWC"),
        feature_group_count=signal.shape[1],
        preferred_element_type=jnp.float32,
    )[0]


def contract(left, right, left_dim, right_dim):
    return lax.dot_general(
        left, right, (((left_dim,), (right_dim,)), ((), ())), preferred_element_type=jnp.float32
    )


def expert_pass(token_rows, scaled_rows, gate_mat, up_mat, down_mat):
    pre_gate = jnp.dot(token_rows, gate_mat, preferred_element_type=jnp.float32)
    pre_up = jnp.dot(token_rows, up_mat, preferred_element_type=jnp.float32)
    sigma = jax.nn.sigmoid(pre_gate)
    swish = pre_gate * sigma
    hidden = (swish * pre_up).astype(jnp.bfloat16)
    outputs = jnp.dot(hidden, down_mat, preferred_element_type=jnp.float32).astype(jnp.bfloat16)
    grad_hidden = contract(scaled_rows, down_mat, 1, 1)
    grad_pre_gate = (grad_hidden * pre_up * (sigma * (1.0 + pre_gate * (1.0 - sigma)))).astype(
        jnp.bfloat16
    )
    grad_pre_up = (grad_hidden * swish).astype(jnp.bfloat16)
    part_gate = contract(token_rows, grad_pre_gate, 0, 0)
    part_up = contract(token_rows, grad_pre_up, 0, 0)
    part_down = contract(hidden, scaled_rows, 0, 0)
    grad_rows = (
        contract(grad_pre_gate, gate_mat, 1, 1) + contract(grad_pre_up, up_mat, 1, 1)
    ).astype(jnp.bfloat16)
    return (grad_rows, outputs, (part_gate, part_up, part_down))


def routed_body(inputs, grad_out, gates, expert_ids, slot_index, filter_taps, w_gate, w_up, w_down):
    tok_count, width = inputs.shape
    taps = filter_taps.shape[0]
    top_count = expert_ids.shape[1]
    experts = lax.axis_size("expert")
    capacity = tok_count * top_count // experts
    reach = taps - 1
    shift_count = (reach + tok_count - 1) // tok_count
    earlier = [from_behind(inputs, "seq", shift_by) for shift_by in range(shift_count, 0, -1)]
    extended = jnp.concatenate(earlier + [inputs], axis=0)[-(tok_count + reach) :]
    filtered = depthwise(extended, filter_taps[::-1]).astype(jnp.bfloat16)
    kept = slot_index < capacity
    dest = jnp.where(kept, expert_ids * capacity + slot_index, experts * capacity).reshape(-1)

    def place(values):
        rest = values.shape[1:]
        empty = jnp.zeros((experts * capacity,) + rest, values.dtype)
        return empty.at[dest].set(values, mode="drop").reshape((experts, capacity) + rest)

    def fetch(buffer):
        rest = buffer.shape[2:]
        flat = buffer.reshape((experts * capacity,) + rest)
        return jnp.take(flat, dest, axis=0, mode="fill", fill_value=0).reshape(
            (tok_count, top_count) + rest
        )

    token_send = place(
        jnp.broadcast_to(filtered[:, None, :], (tok_count, top_count, width)).reshape(-1, width)
    )
    gate_full, up_full, down_full = (
        lax.all_gather(w_gate, "seq", axis=1, tiled=True),
        lax.all_gather(w_up, "seq", axis=1, tiled=True),
        lax.all_gather(w_down, "seq", axis=1, tiled=True),
    )
    gate_mat = gate_full[0]
    up_mat = up_full[0]
    down_mat = down_full[0]
    scaled = (
        gates.astype(jnp.float32)[:, :, None] * grad_out.astype(jnp.float32)[:, None, :]
    ).astype(jnp.bfloat16)
    token_recv, scaled_recv = (
        lax.all_to_all(token_send, "expert", split_axis=0, concat_axis=0, tiled=True),
        lax.all_to_all(
            place(scaled.reshape(-1, width)), "expert", split_axis=0, concat_axis=0, tiled=True
        ),
    )
    grad_rows, outputs, partials = expert_pass(
        token_recv.reshape(-1, width), scaled_recv.reshape(-1, width), gate_mat, up_mat, down_mat
    )
    grad_back, output_back = (
        lax.all_to_all(
            grad_rows.reshape(experts, capacity, width),
            "expert",
            split_axis=0,
            concat_axis=0,
            tiled=True,
        ),
        lax.all_to_all(
            outputs.reshape(experts, capacity, width),
            "expert",
            split_axis=0,
            concat_axis=0,
            tiled=True,
        ),
    )
    output_rows = fetch(output_back)
    grad_gates = jnp.sum(
        grad_out.astype(jnp.float32)[:, None, :] * output_rows.astype(jnp.float32), axis=2
    ).astype(jnp.bfloat16)
    summed_gate, summed_up, summed_down = (
        lax.psum_scatter(
            partials[0][None].astype(jnp.bfloat16), "seq", scatter_dimension=1, tiled=True
        ).astype(jnp.float32),
        lax.psum_scatter(
            partials[1][None].astype(jnp.bfloat16), "seq", scatter_dimension=1, tiled=True
        ).astype(jnp.float32),
        lax.psum_scatter(
            partials[2][None].astype(jnp.bfloat16), "seq", scatter_dimension=1, tiled=True
        ).astype(jnp.float32),
    )
    grad_filtered = jnp.sum(fetch(grad_back).astype(jnp.float32), axis=1).astype(jnp.bfloat16)
    later = [from_behind(grad_filtered, "seq", -shift_by) for shift_by in range(1, shift_count + 1)]
    grad_extended = jnp.concatenate([grad_filtered] + later, axis=0)[: tok_count + reach]
    grad_inputs = depthwise(grad_extended, filter_taps).astype(jnp.bfloat16)
    local_taps = depthwise(extended, grad_filtered)[::-1]
    grad_filter = lax.psum(local_taps, ("expert", "seq"))
    return (
        grad_inputs,
        grad_gates,
        grad_filter,
        summed_gate.astype(jnp.bfloat16),
        summed_up.astype(jnp.bfloat16),
        summed_down.astype(jnp.bfloat16),
    )


def transforms(size):
    freq = 2.0 * np.pi * (np.arange(size // 2) + 0.5) / size
    angle = freq[:, None] * np.arange(size)[None, :]
    forward = np.concatenate([np.cos(angle), np.sin(angle)], axis=0)
    inverse = forward.T * (2.0 / size)

    def pieces(matrix):
        high = matrix.astype(jnp.bfloat16)
        low = (matrix - high.astype(np.float64)).astype(jnp.bfloat16)
        return high, low

    return pieces(forward) + pieces(inverse)


def mm(left, right):
    return jnp.dot(left, right, preferred_element_type=F32)


def dense_kernel(
    rows_ref, cot_ref, gates_ref, ids_ref, slots_ref, wg_ref, wu_ref, wd_ref, taps_ref,
    fh_ref, fl_ref, ih_ref, il_ref,
    gin_ref, gg_ref, gf_ref, dg_ref, du_ref, dd_ref,
    xext, tap_spec, x_spec, tall, gall, wall, hid, gpre, scaled, back, rall,
    part, sib_in, pair, cross_in, gext, gfs, gf_in, gfz, gfz_in, gfull,
    weigh, sums, sums_in,
    send_sem, recv_sem,
):
    z = lax.axis_index("expert")
    q = lax.axis_index("seq")
    tok, width = rows_ref.shape
    size = xext.shape[0]
    half = size // 2
    reach_at = size - tok
    dq = 2 * tok
    ff = hid.shape[1]
    fq = ff // 4
    chunk = 256
    chunks = width // chunk
    sib = q + 1 - 2 * (q % 2)
    cross = (q + 2) % 4
    far = (sib + 2) % 4

    def link(n, src, dst, axis, peer):
        return pltpu.make_async_remote_copy(
            src_ref=src, dst_ref=dst, send_sem=send_sem.at[n], recv_sem=recv_sem.at[n],
            device_id={axis: peer}, device_id_type=MESH,
        )

    barrier = pltpu.get_barrier_semaphore()
    for s in range(1, 4):
        pl.semaphore_signal(barrier, inc=1, device_id={"expert": (z + s) % 4}, device_id_type=MESH)
        pl.semaphore_signal(barrier, inc=1, device_id={"seq": (q + s) % 4}, device_id_type=MESH)
    pl.semaphore_wait(barrier, 6)

    halo = [
        link(n, rows_ref, xext.at[pl.ds(reach_at - (n + 1) * tok, tok)], "seq", (q + n + 1) % 4)
        for n in range(2)
    ]
    for n in range(2):
        @pl.when(q + n + 1 < 4)
        def _(n=n):
            halo[n].start()

        @pl.when(q < n + 1)
        def _(n=n):
            xext[pl.ds(reach_at - (n + 1) * tok, tok)] = jnp.zeros((tok, width), BF16)

    ids = ids_ref[...]
    held = jnp.where(slots_ref[...] < tok, gates_ref[...].astype(F32), 0.0)
    eye = lax.broadcasted_iota(jnp.int32, (tok, tok), 0) == lax.broadcasted_iota(
        jnp.int32, (tok, tok), 1
    )

    def as_row(column):
        return jnp.sum(jnp.where(eye, column, 0.0), axis=0, keepdims=True)

    def as_column(row):
        return jnp.sum(jnp.where(eye, row, 0.0), axis=1, keepdims=True)

    weigh[0] = jnp.zeros(weigh.shape[1:], F32)
    for e in range(4):
        weigh[0, e:e + 1] = as_row(
            jnp.sum(jnp.where(ids == e, held, 0.0), axis=1, keepdims=True)
        )
    weighs = [link(30 + s, weigh.at[0], weigh.at[s], "expert", (z + s) % 4) for s in range(1, 4)]
    for copy in weighs:
        copy.start()
    cots = [link(1 + s, cot_ref, gall.at[s], "expert", (z + s) % 4) for s in range(1, 4)]
    for copy in cots:
        copy.start()
    wall[q, :dq, :ff] = wg_ref[0]
    wall[q, :dq, ff:] = wu_ref[0]
    wall[q, dq:] = wd_ref[0]
    w_sib = link(8, wall.at[q], wall.at[q], "seq", sib)
    w_cross = link(9, wall.at[q], wall.at[q], "seq", cross)
    w_sib.start()
    gall[0] = cot_ref[...]
    xext[pl.ds(reach_at, tok)] = rows_ref[...]

    def cols(c):
        return pl.ds(pl.multiple_of(c * chunk, chunk), chunk)

    def forward(first, count, values):
        span = slice(first, first + count)
        return mm(fh_ref[:, span], values) + mm(fl_ref[:, span], values)

    def backward(first, count, spec):
        span = slice(first, first + count)
        high = spec.astype(BF16)
        low = (spec - high.astype(F32)).astype(BF16)
        return mm(ih_ref[span], high) + mm(il_ref[span], high) + mm(ih_ref[span], low)

    taps = taps_ref.shape[0]

    @pl.loop(0, chunks)
    def _(c):
        tap_spec[:, cols(c)] = forward(0, taps, taps_ref[:, cols(c)])

    for n in range(2):
        @pl.when(q >= n + 1)
        def _(n=n):
            halo[n].wait_recv()

    w_cross.start()

    @pl.loop(0, chunks)
    def _(c):
        spec = forward(0, size, xext[:, cols(c)])
        x_spec[:, cols(c)] = spec
        xc, xs = spec[:half], spec[half:]
        hc, hs = tap_spec[:half, cols(c)], tap_spec[half:, cols(c)]
        prod = jnp.concatenate([xc * hc - xs * hs, xc * hs + xs * hc], axis=0)
        tall[0, :, cols(c)] = backward(reach_at, tok, prod).astype(BF16)

    rows_out = [link(4 + s, tall.at[0], tall.at[s], "expert", (z + s) % 4) for s in range(1, 4)]
    for copy in rows_out:
        copy.start()

    w_cross.wait_recv()
    w_far = link(10, wall.at[cross], wall.at[cross], "seq", sib)
    w_far.start()
    w_sib.wait_recv()
    w_far.wait_recv()

    def turned(left, right):
        return lax.dot_general(left, right, (((1,), (1,)), ((), ())), preferred_element_type=F32)

    sublanes = lax.broadcasted_iota(jnp.int32, weigh.shape[1:], 0)
    gate_sums = [
        link(33 + s, sums.at[s], sums_in.at[s], "expert", (z + 4 - s) % 4) for s in range(1, 4)
    ]
    backs = [
        link(10 + s, back.at[s], rall.at[s], "expert", (z + 4 - s) % 4) for s in range(1, 4)
    ]
    for s in range(4):
        if s:
            weighs[s - 1].wait_recv()
            cots[s - 1].wait_recv()
            rows_out[s - 1].wait_recv()
        span = pl.ds(s * tok, tok)
        pre = mm(tall[s, :, 0:dq], wall[0, :dq, :])
        for k in range(1, 4):
            pre += mm(tall[s, :, k * dq:(k + 1) * dq], wall[k, :dq, :])
        cot = gall[s]
        weight = as_column(
            jnp.sum(jnp.where(sublanes == z, weigh[s], 0.0), axis=0, keepdims=True)
        )
        raw = jnp.concatenate([turned(cot, wall[k, dq:, :]) for k in range(4)], axis=1)
        gate, up = pre[:, :ff], pre[:, ff:]
        sigma = jax.nn.sigmoid(gate)
        swish = gate * sigma
        hidden = (swish * up).astype(BF16)
        gg = jnp.sum(hidden.astype(F32) * raw, axis=1, keepdims=True)
        grad_hidden = raw * weight
        grad_gate = grad_hidden * up * (sigma * (1.0 + gate * (1.0 - sigma)))
        gp = jnp.concatenate([grad_gate.astype(BF16), (grad_hidden * swish).astype(BF16)], axis=1)
        hid[span] = hidden
        gpre[span] = gp
        scaled[span] = (weight * cot.astype(F32)).astype(BF16)
        target = back if s else rall
        for k in range(4):
            target[s, :, k * dq:(k + 1) * dq] = turned(gp, wall[k, :dq, :]).astype(BF16)
        (sums if s else sums_in)[s] = jnp.broadcast_to(as_row(gg), sums.shape[1:])
        if s:
            gate_sums[s - 1].start()
            backs[s - 1].start()

    def across(left, right):
        return lax.dot_general(left, right, (((0,), (0,)), ((), ())), preferred_element_type=F32)

    def partial(slot, dest):
        top = jnp.zeros((dq, 2 * ff), F32)
        low = jnp.zeros((fq, width), F32)
        wide = pl.ds(pl.multiple_of(dest * dq, dq), dq)
        thin = pl.ds(pl.multiple_of(dest * fq, fq), fq)
        for s in range(4):
            top += across(tall[s, :, wide], gpre[pl.ds(s * tok, tok)])
        low = across(hid[:, thin], scaled[...])
        part[slot, :dq] = top.astype(BF16)
        part[slot, dq:] = low.astype(BF16)

    to_sib = [link(14 + n, part.at[n], sib_in.at[n], "seq", sib) for n in range(2)]
    partial(0, far)
    to_sib[0].start()
    partial(1, sib)
    to_sib[1].start()
    partial(2, cross)
    to_sib[0].wait_recv()
    pair[...] = (part[2].astype(F32) + sib_in[0].astype(F32)).astype(BF16)
    to_cross = link(16, pair, cross_in, "seq", cross)
    to_cross.start()
    partial(3, q)

    for copy in backs:
        copy.wait_recv()
    total = jnp.zeros((tok, width), F32)
    for s in range(4):
        total += rall[s].astype(F32)
    gext[pl.ds(0, tok)] = total.astype(BF16)
    halo_back = [
        link(17 + n, gext.at[pl.ds(0, tok)], gext.at[pl.ds((n + 1) * tok, tok)], "seq", (q + 3 - n) % 4)
        for n in range(2)
    ]
    for n in range(2):
        @pl.when(q >= n + 1)
        def _(n=n):
            halo_back[n].start()

        @pl.when(q + n + 1 >= 4)
        def _(n=n):
            gext[pl.ds((n + 1) * tok, tok)] = jnp.zeros((tok, width), BF16)

    for copy in gate_sums:
        copy.wait_recv()
    gate_grads = jnp.zeros(ids.shape, F32)
    for s in range(4):
        gate_grads += jnp.where(ids == (z + s) % 4, as_column(sums_in[s, 0:1]), 0.0)
    gg_ref[...] = jnp.where(slots_ref[...] < tok, gate_grads, 0.0).astype(BF16)

    quarter = taps // 4

    @pl.loop(0, chunks)
    def _(c):
        spec = forward(reach_at, tok, gext[pl.ds(0, tok), cols(c)])
        gc, gs = spec[:half], spec[half:]
        xc, xs = x_spec[:half, cols(c)], x_spec[half:, cols(c)]
        prod = jnp.concatenate([gc * xc + gs * xs, gs * xc - gc * xs], axis=0)
        result = backward(0, taps, prod).astype(BF16)
        for k in range(4):
            gfs[k, :, cols(c)] = result[k * quarter:(k + 1) * quarter]

    gf_seq = [
        link(18 + s, gfs.at[(q + s) % 4], gf_in.at[s], "seq", (q + s) % 4) for s in range(1, 4)
    ]
    for copy in gf_seq:
        copy.start()

    for copy in gf_seq:
        copy.wait_recv()
    mine = gfs[q].astype(F32)
    for s in range(1, 4):
        mine += gf_in[s].astype(F32)
    piece = quarter // 4
    for k in range(4):
        gfz[k] = mine[k * piece:(k + 1) * piece].astype(BF16)
    gf_exp = [
        link(21 + s, gfz.at[(z + s) % 4], gfz_in.at[s], "expert", (z + s) % 4) for s in range(1, 4)
    ]
    for copy in gf_exp:
        copy.start()

    for n in range(2):
        @pl.when(q + n + 1 < 4)
        def _(n=n):
            halo_back[n].wait_recv()

    for copy in gf_exp:
        copy.wait_recv()
    mine = gfz[z].astype(F32)
    for s in range(1, 4):
        mine += gfz_in[s].astype(F32)
    gfull[q, z] = mine.astype(BF16)
    gf_out = [
        link(24 + s, gfull.at[q, z], gfull.at[q, z], "expert", (z + s) % 4) for s in range(1, 4)
    ]
    for copy in gf_out:
        copy.start()

    @pl.loop(0, chunks)
    def _(c):
        spec = forward(0, size, gext[:, cols(c)])
        gc, gs = spec[:half], spec[half:]
        hc, hs = tap_spec[:half, cols(c)], tap_spec[half:, cols(c)]
        prod = jnp.concatenate([gc * hc + gs * hs, gs * hc - gc * hs], axis=0)
        gin_ref[:, cols(c)] = backward(0, tok, prod).astype(BF16)

    for copy in gf_out:
        copy.wait_recv()
    gf_last = [link(27 + s, gfull.at[q], gfull.at[q], "seq", (q + s) % 4) for s in range(1, 4)]
    for copy in gf_last:
        copy.start()

    to_sib[1].wait_recv()
    to_cross.wait_recv()
    weights = (
        part[3].astype(F32) + sib_in[1].astype(F32) + cross_in[...].astype(F32)
    ).astype(BF16)
    dg_ref[0] = weights[:dq, :ff]
    du_ref[0] = weights[:dq, ff:]
    dd_ref[0] = weights[dq:]

    for copy in gf_last:
        copy.wait_recv()
    for a in range(4):
        for b in range(4):
            gf_ref[pl.ds((a * 4 + b) * piece, piece)] = gfull[a, b].astype(F32)

    for n in range(2):
        @pl.when(q + n + 1 < 4)
        def _(n=n):
            halo[n].wait_send()

        @pl.when(q >= n + 1)
        def _(n=n):
            halo_back[n].wait_send()
    for copy in (
        weighs + gate_sums + cots + [w_sib, w_cross, w_far] + rows_out + backs + to_sib + [to_cross]
        + gf_seq + gf_exp + gf_out + gf_last
    ):
        copy.wait_send()


def dense_body(inputs, grad_out, gates, expert_ids, slot_index, filter_taps, w_gate, w_up, w_down):
    tok, width = inputs.shape
    taps = filter_taps.shape[0]
    ff = w_gate.shape[2]
    size = taps + tok
    rows = w_gate.shape[1] + w_down.shape[1]
    vm = lambda *shape: pltpu.VMEM(shape, BF16)
    return pl.pallas_call(
        dense_kernel,
        out_shape=(
            jax.ShapeDtypeStruct((tok, width), BF16),
            jax.ShapeDtypeStruct(gates.shape, BF16),
            jax.ShapeDtypeStruct((taps, width), F32),
            jax.ShapeDtypeStruct(w_gate.shape, BF16),
            jax.ShapeDtypeStruct(w_up.shape, BF16),
            jax.ShapeDtypeStruct(w_down.shape, BF16),
        ),
        in_specs=[pl.BlockSpec(memory_space=pltpu.VMEM)] * 13,
        out_specs=(pl.BlockSpec(memory_space=pltpu.VMEM),) * 6,
        scratch_shapes=[
            vm(size, width), pltpu.VMEM((size, width), F32), pltpu.VMEM((size, width), F32),
            vm(4, tok, width), vm(4, tok, width), vm(4, rows, width),
            vm(4 * tok, ff), vm(4 * tok, 2 * ff), vm(4 * tok, width),
            vm(4, tok, width), vm(4, tok, width),
            vm(4, rows, width), vm(2, rows, width), vm(rows, width), vm(rows, width),
            vm(size, width), vm(4, taps // 4, width), vm(4, taps // 4, width),
            vm(4, taps // 16, width), vm(4, taps // 16, width),
            vm(4, 4, taps // 16, width),
            pltpu.VMEM((4, 8, tok), F32), pltpu.VMEM((4, 8, tok), F32), pltpu.VMEM((4, 8, tok), F32),
            pltpu.SemaphoreType.DMA((37,)), pltpu.SemaphoreType.DMA((37,)),
        ],
        compiler_params=pltpu.CompilerParams(
            collective_id=0, has_side_effects=True, vmem_limit_bytes=52 * 1024 * 1024
        ),
    )(
        inputs, grad_out, gates, expert_ids, slot_index, w_gate, w_up, w_down, filter_taps,
        *[jnp.asarray(m) for m in transforms(size)],
    )


def body_of(mesh):
    def body(*args):
        top_count = args[3].shape[1]
        tok, taps, dq = args[0].shape[0], args[5].shape[0], args[6].shape[1]
        small = mesh.shape["expert"] == top_count == 4 and mesh.shape["seq"] == 4
        if small and tok == 128 and taps == 2 * tok and dq == 2 * tok and 2 * args[6].shape[2] == args[0].shape[1]:
            return dense_body(*args)
        return routed_body(*args)

    return body


def solution(mesh):
    return jax.shard_map(
        body_of(mesh),
        mesh=mesh,
        in_specs=(
            P(("groups", "expert", "seq"), None),
            P(("groups", "expert", "seq"), None),
            P(("groups", "expert", "seq"), None),
            P(("groups", "expert", "seq"), None),
            P(("groups", "expert", "seq"), None),
            P(),
            P("expert", "seq", None),
            P("expert", "seq", None),
            P("expert", "seq", None),
        ),
        out_specs=(
            P(("groups", "expert", "seq"), None),
            P(("groups", "expert", "seq"), None),
            P("groups", None),
            P(("groups", "expert"), "seq", None),
            P(("groups", "expert"), "seq", None),
            P(("groups", "expert"), "seq", None),
        ),
        check_vma=False,
    )
```

```python
import functools

import jax
import jax.numpy as jnp
import numpy as np
from jax import lax
from jax.experimental import pallas as pl
from jax.experimental.pallas import tpu as pltpu
from jax.sharding import PartitionSpec as P

MESH = pl.DeviceIdType.MESH
F32 = jnp.float32
BF16 = jnp.bfloat16


def from_behind(block, axis, distance):
    devices = range(lax.axis_size(axis))
    route = [(i - distance, i) for i in devices if i - distance in devices]
    return lax.ppermute(block, axis, route)


def depthwise(signal, kernel):
    return lax.conv_general_dilated(
        signal[None],
        kernel[:, None, :],
        (1,),
        "VALID",
        dimension_numbers=("NWC", "WIO", "NWC"),
        feature_group_count=signal.shape[1],
        preferred_element_type=jnp.float32,
    )[0]


def contract(left, right, left_dim, right_dim):
    return lax.dot_general(
        left, right, (((left_dim,), (right_dim,)), ((), ())), preferred_element_type=jnp.float32
    )


def expert_pass(token_rows, scaled_rows, gate_mat, up_mat, down_mat):
    pre_gate = jnp.dot(token_rows, gate_mat, preferred_element_type=jnp.float32)
    pre_up = jnp.dot(token_rows, up_mat, preferred_element_type=jnp.float32)
    sigma = jax.nn.sigmoid(pre_gate)
    swish = pre_gate * sigma
    hidden = (swish * pre_up).astype(jnp.bfloat16)
    outputs = jnp.dot(hidden, down_mat, preferred_element_type=jnp.float32).astype(jnp.bfloat16)
    grad_hidden = contract(scaled_rows, down_mat, 1, 1)
    grad_pre_gate = (grad_hidden * pre_up * (sigma * (1.0 + pre_gate * (1.0 - sigma)))).astype(
        jnp.bfloat16
    )
    grad_pre_up = (grad_hidden * swish).astype(jnp.bfloat16)
    part_gate = contract(token_rows, grad_pre_gate, 0, 0)
    part_up = contract(token_rows, grad_pre_up, 0, 0)
    part_down = contract(hidden, scaled_rows, 0, 0)
    grad_rows = (
        contract(grad_pre_gate, gate_mat, 1, 1) + contract(grad_pre_up, up_mat, 1, 1)
    ).astype(jnp.bfloat16)
    return (grad_rows, outputs, (part_gate, part_up, part_down))


def routed_body(inputs, grad_out, gates, expert_ids, slot_index, filter_taps, w_gate, w_up, w_down):
    tok_count, width = inputs.shape
    taps = filter_taps.shape[0]
    top_count = expert_ids.shape[1]
    experts = lax.axis_size("expert")
    capacity = tok_count * top_count // experts
    reach = taps - 1
    shift_count = (reach + tok_count - 1) // tok_count
    earlier = [from_behind(inputs, "seq", shift_by) for shift_by in range(shift_count, 0, -1)]
    extended = jnp.concatenate(earlier + [inputs], axis=0)[-(tok_count + reach) :]
    filtered = depthwise(extended, filter_taps[::-1]).astype(jnp.bfloat16)
    kept = slot_index < capacity
    dest = jnp.where(kept, expert_ids * capacity + slot_index, experts * capacity).reshape(-1)

    def place(values):
        rest = values.shape[1:]
        empty = jnp.zeros((experts * capacity,) + rest, values.dtype)
        return empty.at[dest].set(values, mode="drop").reshape((experts, capacity) + rest)

    def fetch(buffer):
        rest = buffer.shape[2:]
        flat = buffer.reshape((experts * capacity,) + rest)
        return jnp.take(flat, dest, axis=0, mode="fill", fill_value=0).reshape(
            (tok_count, top_count) + rest
        )

    token_send = place(
        jnp.broadcast_to(filtered[:, None, :], (tok_count, top_count, width)).reshape(-1, width)
    )
    gate_full, up_full, down_full = (
        lax.all_gather(w_gate, "seq", axis=1, tiled=True),
        lax.all_gather(w_up, "seq", axis=1, tiled=True),
        lax.all_gather(w_down, "seq", axis=1, tiled=True),
    )
    gate_mat = gate_full[0]
    up_mat = up_full[0]
    down_mat = down_full[0]
    scaled = (
        gates.astype(jnp.float32)[:, :, None] * grad_out.astype(jnp.float32)[:, None, :]
    ).astype(jnp.bfloat16)
    token_recv, scaled_recv = (
        lax.all_to_all(token_send, "expert", split_axis=0, concat_axis=0, tiled=True),
        lax.all_to_all(
            place(scaled.reshape(-1, width)), "expert", split_axis=0, concat_axis=0, tiled=True
        ),
    )
    grad_rows, outputs, partials = expert_pass(
        token_recv.reshape(-1, width), scaled_recv.reshape(-1, width), gate_mat, up_mat, down_mat
    )
    grad_back, output_back = (
        lax.all_to_all(
            grad_rows.reshape(experts, capacity, width),
            "expert",
            split_axis=0,
            concat_axis=0,
            tiled=True,
        ),
        lax.all_to_all(
            outputs.reshape(experts, capacity, width),
            "expert",
            split_axis=0,
            concat_axis=0,
            tiled=True,
        ),
    )
    output_rows = fetch(output_back)
    grad_gates = jnp.sum(
        grad_out.astype(jnp.float32)[:, None, :] * output_rows.astype(jnp.float32), axis=2
    ).astype(jnp.bfloat16)
    summed_gate, summed_up, summed_down = (
        lax.psum_scatter(
            partials[0][None].astype(jnp.bfloat16), "seq", scatter_dimension=1, tiled=True
        ).astype(jnp.float32),
        lax.psum_scatter(
            partials[1][None].astype(jnp.bfloat16), "seq", scatter_dimension=1, tiled=True
        ).astype(jnp.float32),
        lax.psum_scatter(
            partials[2][None].astype(jnp.bfloat16), "seq", scatter_dimension=1, tiled=True
        ).astype(jnp.float32),
    )
    grad_filtered = jnp.sum(fetch(grad_back).astype(jnp.float32), axis=1).astype(jnp.bfloat16)
    later = [from_behind(grad_filtered, "seq", -shift_by) for shift_by in range(1, shift_count + 1)]
    grad_extended = jnp.concatenate([grad_filtered] + later, axis=0)[: tok_count + reach]
    grad_inputs = depthwise(grad_extended, filter_taps).astype(jnp.bfloat16)
    local_taps = depthwise(extended, grad_filtered)[::-1]
    grad_filter = lax.psum(local_taps, ("expert", "seq"))
    return (
        grad_inputs,
        grad_gates,
        grad_filter,
        summed_gate.astype(jnp.bfloat16),
        summed_up.astype(jnp.bfloat16),
        summed_down.astype(jnp.bfloat16),
    )


def transforms(size):
    freq = 2.0 * np.pi * (np.arange(size // 2) + 0.5) / size
    angle = freq[:, None] * np.arange(size)[None, :]
    forward = np.concatenate([np.cos(angle), np.sin(angle)], axis=0)
    inverse = forward.T * (2.0 / size)

    def pieces(matrix):
        high = matrix.astype(jnp.bfloat16)
        low = (matrix - high.astype(np.float64)).astype(jnp.bfloat16)
        return high, low

    return pieces(forward) + pieces(inverse)


def mm(left, right):
    return jnp.dot(left, right, preferred_element_type=F32)


def dense_kernel(
    rows_ref, cot_ref, gates_ref, ids_ref, slots_ref, wg_ref, wu_ref, wd_ref, taps_ref,
    fh_ref, fl_ref, ih_ref, il_ref,
    gin_ref, gg_ref, gf_ref, dg_ref, du_ref, dd_ref,
    xext, tap_spec, x_spec, tall, gall, wall, hid, gpre, scaled, back, rall,
    part, sib_in, pair, cross_in, gext, gfs, gf_in, gfz, gfz_in, gfull,
    weigh, sums, sums_in,
    send_sem, recv_sem,
):
    z = lax.axis_index("expert")
    q = lax.axis_index("seq")
    tok, width = rows_ref.shape
    size = xext.shape[0]
    half = size // 2
    reach_at = size - tok
    dq = 2 * tok
    ff = hid.shape[1]
    fq = ff // 4
    chunk = 256
    chunks = width // chunk
    sib = q + 1 - 2 * (q % 2)
    cross = (q + 2) % 4
    far = (sib + 2) % 4

    def link(n, src, dst, axis, peer, arrival=None):
        return pltpu.make_async_remote_copy(
            src_ref=src, dst_ref=dst, send_sem=send_sem.at[n],
            recv_sem=recv_sem.at[n if arrival is None else arrival],
            device_id={axis: peer}, device_id_type=MESH,
        )

    def pick(a, b, c, d):
        return jnp.where(z == 0, a, jnp.where(z == 1, b, jnp.where(z == 2, c, d)))

    def hop(base, buf, origin, step):
        return link(
            base + (0 if step > 0 else 4) + origin, buf.at[origin], buf.at[origin],
            "expert", (z + 4 + step) % 4, base + origin,
        )

    def spread(base, buf, distance, send=True):
        for step in (1, -1):
            origin = z - step * distance
            has_origin = origin >= 0 if step > 0 else origin <= 3
            has_next = z < 3 if step > 0 else z > 0

            @pl.when(has_origin)
            def _(origin=origin, has_next=has_next, step=step):
                if distance and send:
                    hop(base, buf, origin, step).wait_recv()

                @pl.when(has_next)
                def _():
                    if send:
                        hop(base, buf, origin, step).start()
                    else:
                        hop(base, buf, origin, step).wait_send()

    barrier = pltpu.get_barrier_semaphore()
    for s in range(1, 4):
        pl.semaphore_signal(barrier, inc=1, device_id={"expert": (z + s) % 4}, device_id_type=MESH)
        pl.semaphore_signal(barrier, inc=1, device_id={"seq": (q + s) % 4}, device_id_type=MESH)
    pl.semaphore_wait(barrier, 6)

    halo = [
        link(n, rows_ref, xext.at[pl.ds(reach_at - (n + 1) * tok, tok)], "seq", (q + n + 1) % 4)
        for n in range(2)
    ]
    for n in range(2):
        @pl.when(q + n + 1 < 4)
        def _(n=n):
            halo[n].start()

        @pl.when(q < n + 1)
        def _(n=n):
            xext[pl.ds(reach_at - (n + 1) * tok, tok)] = jnp.zeros((tok, width), BF16)

    ids = ids_ref[...]
    held = jnp.where(slots_ref[...] < tok, gates_ref[...].astype(F32), 0.0)
    eye = lax.broadcasted_iota(jnp.int32, (tok, tok), 0) == lax.broadcasted_iota(
        jnp.int32, (tok, tok), 1
    )

    def as_row(column):
        return jnp.sum(jnp.where(eye, column, 0.0), axis=0, keepdims=True)

    def as_column(row):
        return jnp.sum(jnp.where(eye, row, 0.0), axis=1, keepdims=True)

    weigh[z] = jnp.zeros(weigh.shape[1:], F32)
    for e in range(4):
        weigh[z, e:e + 1] = as_row(
            jnp.sum(jnp.where(ids == e, held, 0.0), axis=1, keepdims=True)
        )
    weighs = [
        link(30 + s, weigh.at[z], weigh.at[z], "expert", (z + s) % 4, 61 + z) for s in range(1, 4)
    ]
    for copy in weighs:
        copy.start()
    gall[z] = cot_ref[...]
    spread(37, gall, 0)
    wall[q, :dq, :ff] = wg_ref[0]
    wall[q, :dq, ff:] = wu_ref[0]
    wall[q, dq:] = wd_ref[0]
    w_sib = link(8, wall.at[q], wall.at[q], "seq", sib)
    w_cross = link(9, wall.at[q], wall.at[q], "seq", cross)
    w_sib.start()
    xext[pl.ds(reach_at, tok)] = rows_ref[...]

    def cols(c):
        return pl.ds(pl.multiple_of(c * chunk, chunk), chunk)

    def forward(first, count, values):
        span = slice(first, first + count)
        return mm(fh_ref[:, span], values) + mm(fl_ref[:, span], values)

    def backward(first, count, spec):
        span = slice(first, first + count)
        high = spec.astype(BF16)
        low = (spec - high.astype(F32)).astype(BF16)
        return mm(ih_ref[span], high) + mm(il_ref[span], high) + mm(ih_ref[span], low)

    taps = taps_ref.shape[0]

    @pl.loop(0, chunks)
    def _(c):
        tap_spec[:, cols(c)] = forward(0, taps, taps_ref[:, cols(c)])

    spread(37, gall, 1)
    for n in range(2):
        @pl.when(q >= n + 1)
        def _(n=n):
            halo[n].wait_recv()

    w_cross.start()

    @pl.loop(0, chunks)
    def _(c):
        spec = forward(0, size, xext[:, cols(c)])
        x_spec[:, cols(c)] = spec
        xc, xs = spec[:half], spec[half:]
        hc, hs = tap_spec[:half, cols(c)], tap_spec[half:, cols(c)]
        prod = jnp.concatenate([xc * hc - xs * hs, xc * hs + xs * hc], axis=0)
        tall[z, :, cols(c)] = backward(reach_at, tok, prod).astype(BF16)

    spread(45, tall, 0)
    spread(37, gall, 2)
    spread(45, tall, 1)

    w_cross.wait_recv()
    w_far = link(10, wall.at[cross], wall.at[cross], "seq", sib)
    w_far.start()
    w_sib.wait_recv()
    w_far.wait_recv()

    def turned(left, right):
        return lax.dot_general(left, right, (((1,), (1,)), ((), ())), preferred_element_type=F32)

    origins = [z, pick(1, 0, 1, 2), pick(2, 2, 3, 1), pick(3, 3, 0, 0)]
    sublanes = lax.broadcasted_iota(jnp.int32, weigh.shape[1:], 0)
    gate_sums = [
        link(33 + s, sums.at[s], sums_in.at[z], "expert", origins[s], 57 + z)
        for s in range(1, 4)
    ]
    backs = [
        link(10 + s, back.at[s], rall.at[z], "expert", origins[s], 53 + z) for s in range(1, 4)
    ]
    for s in range(4):
        origin = origins[s]
        if s == 1:
            spread(37, gall, 3)
            for k in range(1, 4):
                peer = (z + k) % 4
                link(30 + k, weigh.at[peer], weigh.at[peer], "expert", peer, 61 + peer).wait_recv()
        elif s > 1:
            spread(45, tall, s)
        span = pl.ds(s * tok, tok)
        pre = mm(tall[origin, :, 0:dq], wall[0, :dq, :])
        for k in range(1, 4):
            pre += mm(tall[origin, :, k * dq:(k + 1) * dq], wall[k, :dq, :])
        cot = gall[origin]
        weight = as_column(
            jnp.sum(jnp.where(sublanes == z, weigh[origin], 0.0), axis=0, keepdims=True)
        )
        raw = jnp.concatenate([turned(cot, wall[k, dq:, :]) for k in range(4)], axis=1)
        gate, up = pre[:, :ff], pre[:, ff:]
        sigma = jax.nn.sigmoid(gate)
        swish = gate * sigma
        hidden = (swish * up).astype(BF16)
        gg = jnp.sum(hidden.astype(F32) * raw, axis=1, keepdims=True)
        grad_hidden = raw * weight
        grad_gate = grad_hidden * up * (sigma * (1.0 + gate * (1.0 - sigma)))
        gp = jnp.concatenate([grad_gate.astype(BF16), (grad_hidden * swish).astype(BF16)], axis=1)
        hid[span] = hidden
        gpre[span] = gp
        scaled[span] = (weight * cot.astype(F32)).astype(BF16)
        target, at = (back, s) if s else (rall, z)
        for k in range(4):
            target[at, :, k * dq:(k + 1) * dq] = turned(gp, wall[k, :dq, :]).astype(BF16)
        (sums if s else sums_in)[at] = jnp.broadcast_to(as_row(gg), sums.shape[1:])
        if s:
            gate_sums[s - 1].start()
            backs[s - 1].start()

    def across(left, right):
        return lax.dot_general(left, right, (((0,), (0,)), ((), ())), preferred_element_type=F32)

    def partial(slot, dest):
        top = jnp.zeros((dq, 2 * ff), F32)
        low = jnp.zeros((fq, width), F32)
        wide = pl.ds(pl.multiple_of(dest * dq, dq), dq)
        thin = pl.ds(pl.multiple_of(dest * fq, fq), fq)
        for s in range(4):
            top += across(tall[origins[s], :, wide], gpre[pl.ds(s * tok, tok)])
        low = across(hid[:, thin], scaled[...])
        part[slot, :dq] = top.astype(BF16)
        part[slot, dq:] = low.astype(BF16)

    to_sib = [link(14 + n, part.at[n], sib_in.at[n], "seq", sib) for n in range(2)]
    partial(0, far)
    to_sib[0].start()
    partial(1, sib)
    to_sib[1].start()
    partial(2, cross)
    to_sib[0].wait_recv()
    pair[...] = (part[2].astype(F32) + sib_in[0].astype(F32)).astype(BF16)
    to_cross = link(16, pair, cross_in, "seq", cross)
    to_cross.start()
    partial(3, q)

    for s in range(1, 4):
        peer = (z + s) % 4
        link(10 + s, back.at[s], rall.at[peer], "expert", peer, 53 + peer).wait_recv()
    total = jnp.zeros((tok, width), F32)
    for s in range(4):
        total += rall[s].astype(F32)
    gext[pl.ds(0, tok)] = total.astype(BF16)
    halo_back = [
        link(17 + n, gext.at[pl.ds(0, tok)], gext.at[pl.ds((n + 1) * tok, tok)], "seq", (q + 3 - n) % 4)
        for n in range(2)
    ]
    for n in range(2):
        @pl.when(q >= n + 1)
        def _(n=n):
            halo_back[n].start()

        @pl.when(q + n + 1 >= 4)
        def _(n=n):
            gext[pl.ds((n + 1) * tok, tok)] = jnp.zeros((tok, width), BF16)

    for s in range(1, 4):
        peer = (z + s) % 4
        link(33 + s, sums.at[s], sums_in.at[peer], "expert", peer, 57 + peer).wait_recv()
    gate_grads = jnp.zeros(ids.shape, F32)
    for s in range(4):
        gate_grads += jnp.where(ids == s, as_column(sums_in[s, 0:1]), 0.0)
    gg_ref[...] = jnp.where(slots_ref[...] < tok, gate_grads, 0.0).astype(BF16)

    quarter = taps // 4

    @pl.loop(0, chunks)
    def _(c):
        spec = forward(reach_at, tok, gext[pl.ds(0, tok), cols(c)])
        gc, gs = spec[:half], spec[half:]
        xc, xs = x_spec[:half, cols(c)], x_spec[half:, cols(c)]
        prod = jnp.concatenate([gc * xc + gs * xs, gs * xc - gc * xs], axis=0)
        result = backward(0, taps, prod).astype(BF16)
        for k in range(4):
            gfs[k, :, cols(c)] = result[k * quarter:(k + 1) * quarter]

    gf_seq = [
        link(18 + s, gfs.at[(q + s) % 4], gf_in.at[s], "seq", (q + s) % 4) for s in range(1, 4)
    ]
    for copy in gf_seq:
        copy.start()

    for copy in gf_seq:
        copy.wait_recv()
    mine = gfs[q].astype(F32)
    for s in range(1, 4):
        mine += gf_in[s].astype(F32)
    piece = quarter // 4
    for k in range(4):
        gfz[k] = mine[k * piece:(k + 1) * piece].astype(BF16)
    gf_exp = [
        link(21 + s, gfz.at[(z + s) % 4], gfz_in.at[s], "expert", (z + s) % 4) for s in range(1, 4)
    ]
    for copy in gf_exp:
        copy.start()

    for n in range(2):
        @pl.when(q + n + 1 < 4)
        def _(n=n):
            halo_back[n].wait_recv()

    for copy in gf_exp:
        copy.wait_recv()
    mine = gfz[z].astype(F32)
    for s in range(1, 4):
        mine += gfz_in[s].astype(F32)
    gfull[q, z] = mine.astype(BF16)
    gf_out = [
        link(24 + s, gfull.at[q, z], gfull.at[q, z], "expert", (z + s) % 4) for s in range(1, 4)
    ]
    for copy in gf_out:
        copy.start()

    @pl.loop(0, chunks)
    def _(c):
        spec = forward(0, size, gext[:, cols(c)])
        gc, gs = spec[:half], spec[half:]
        hc, hs = tap_spec[:half, cols(c)], tap_spec[half:, cols(c)]
        prod = jnp.concatenate([gc * hc + gs * hs, gs * hc - gc * hs], axis=0)
        gin_ref[:, cols(c)] = backward(0, tok, prod).astype(BF16)

    for copy in gf_out:
        copy.wait_recv()
    gf_last = [link(27 + s, gfull.at[q], gfull.at[q], "seq", (q + s) % 4) for s in range(1, 4)]
    for copy in gf_last:
        copy.start()

    to_sib[1].wait_recv()
    to_cross.wait_recv()
    weights = (
        part[3].astype(F32) + sib_in[1].astype(F32) + cross_in[...].astype(F32)
    ).astype(BF16)
    dg_ref[0] = weights[:dq, :ff]
    du_ref[0] = weights[:dq, ff:]
    dd_ref[0] = weights[dq:]

    for copy in gf_last:
        copy.wait_recv()
    for a in range(4):
        for b in range(4):
            gf_ref[pl.ds((a * 4 + b) * piece, piece)] = gfull[a, b].astype(F32)

    for n in range(2):
        @pl.when(q + n + 1 < 4)
        def _(n=n):
            halo[n].wait_send()

        @pl.when(q >= n + 1)
        def _(n=n):
            halo_back[n].wait_send()
    for d in range(3):
        spread(37, gall, d, False)
        spread(45, tall, d, False)
    for copy in (
        weighs + gate_sums + [w_sib, w_cross, w_far] + backs + to_sib + [to_cross]
        + gf_seq + gf_exp + gf_out + gf_last
    ):
        copy.wait_send()


def dense_body(inputs, grad_out, gates, expert_ids, slot_index, filter_taps, w_gate, w_up, w_down):
    tok, width = inputs.shape
    taps = filter_taps.shape[0]
    ff = w_gate.shape[2]
    size = taps + tok
    rows = w_gate.shape[1] + w_down.shape[1]
    vm = lambda *shape: pltpu.VMEM(shape, BF16)
    return pl.pallas_call(
        dense_kernel,
        out_shape=(
            jax.ShapeDtypeStruct((tok, width), BF16),
            jax.ShapeDtypeStruct(gates.shape, BF16),
            jax.ShapeDtypeStruct((taps, width), F32),
            jax.ShapeDtypeStruct(w_gate.shape, BF16),
            jax.ShapeDtypeStruct(w_up.shape, BF16),
            jax.ShapeDtypeStruct(w_down.shape, BF16),
        ),
        in_specs=[pl.BlockSpec(memory_space=pltpu.VMEM)] * 13,
        out_specs=(pl.BlockSpec(memory_space=pltpu.VMEM),) * 6,
        scratch_shapes=[
            vm(size, width), pltpu.VMEM((size, width), F32), pltpu.VMEM((size, width), F32),
            vm(4, tok, width), vm(4, tok, width), vm(4, rows, width),
            vm(4 * tok, ff), vm(4 * tok, 2 * ff), vm(4 * tok, width),
            vm(4, tok, width), vm(4, tok, width),
            vm(4, rows, width), vm(2, rows, width), vm(rows, width), vm(rows, width),
            vm(size, width), vm(4, taps // 4, width), vm(4, taps // 4, width),
            vm(4, taps // 16, width), vm(4, taps // 16, width),
            vm(4, 4, taps // 16, width),
            pltpu.VMEM((4, 8, tok), F32), pltpu.VMEM((4, 8, tok), F32), pltpu.VMEM((4, 8, tok), F32),
            pltpu.SemaphoreType.DMA((65,)), pltpu.SemaphoreType.DMA((65,)),
        ],
        compiler_params=pltpu.CompilerParams(
            collective_id=0, has_side_effects=True, vmem_limit_bytes=52 * 1024 * 1024
        ),
    )(
        inputs, grad_out, gates, expert_ids, slot_index, w_gate, w_up, w_down, filter_taps,
        *[jnp.asarray(m) for m in transforms(size)],
    )


def body_of(mesh):
    def body(*args):
        top_count = args[3].shape[1]
        tok, taps, dq = args[0].shape[0], args[5].shape[0], args[6].shape[1]
        small = mesh.shape["expert"] == top_count == 4 and mesh.shape["seq"] == 4
        if small and tok == 128 and taps == 2 * tok and dq == 2 * tok and 2 * args[6].shape[2] == args[0].shape[1]:
            return dense_body(*args)
        return routed_body(*args)

    return body


def solution(mesh):
    return jax.shard_map(
        body_of(mesh),
        mesh=mesh,
        in_specs=(
            P(("groups", "expert", "seq"), None),
            P(("groups", "expert", "seq"), None),
            P(("groups", "expert", "seq"), None),
            P(("groups", "expert", "seq"), None),
            P(("groups", "expert", "seq"), None),
            P(),
            P("expert", "seq", None),
            P("expert", "seq", None),
            P("expert", "seq", None),
        ),
        out_specs=(
            P(("groups", "expert", "seq"), None),
            P(("groups", "expert", "seq"), None),
            P("groups", None),
            P(("groups", "expert"), "seq", None),
            P(("groups", "expert"), "seq", None),
            P(("groups", "expert"), "seq", None),
        ),
        check_vma=False,
    )
```

```python
import functools

import jax
import jax.numpy as jnp
import numpy as np
from jax import lax
from jax.experimental import pallas as pl
from jax.experimental.pallas import tpu as pltpu
from jax.sharding import PartitionSpec as P

MESH = pl.DeviceIdType.MESH
F32 = jnp.float32
BF16 = jnp.bfloat16


def from_behind(block, axis, distance):
    devices = range(lax.axis_size(axis))
    route = [(i - distance, i) for i in devices if i - distance in devices]
    return lax.ppermute(block, axis, route)


def depthwise(signal, kernel):
    return lax.conv_general_dilated(
        signal[None],
        kernel[:, None, :],
        (1,),
        "VALID",
        dimension_numbers=("NWC", "WIO", "NWC"),
        feature_group_count=signal.shape[1],
        preferred_element_type=jnp.float32,
    )[0]


def contract(left, right, left_dim, right_dim):
    return lax.dot_general(
        left, right, (((left_dim,), (right_dim,)), ((), ())), preferred_element_type=jnp.float32
    )


def expert_pass(token_rows, scaled_rows, gate_mat, up_mat, down_mat):
    pre_gate = jnp.dot(token_rows, gate_mat, preferred_element_type=jnp.float32)
    pre_up = jnp.dot(token_rows, up_mat, preferred_element_type=jnp.float32)
    sigma = jax.nn.sigmoid(pre_gate)
    swish = pre_gate * sigma
    hidden = (swish * pre_up).astype(jnp.bfloat16)
    outputs = jnp.dot(hidden, down_mat, preferred_element_type=jnp.float32).astype(jnp.bfloat16)
    grad_hidden = contract(scaled_rows, down_mat, 1, 1)
    grad_pre_gate = (grad_hidden * pre_up * (sigma * (1.0 + pre_gate * (1.0 - sigma)))).astype(
        jnp.bfloat16
    )
    grad_pre_up = (grad_hidden * swish).astype(jnp.bfloat16)
    part_gate = contract(token_rows, grad_pre_gate, 0, 0)
    part_up = contract(token_rows, grad_pre_up, 0, 0)
    part_down = contract(hidden, scaled_rows, 0, 0)
    grad_rows = (
        contract(grad_pre_gate, gate_mat, 1, 1) + contract(grad_pre_up, up_mat, 1, 1)
    ).astype(jnp.bfloat16)
    return (grad_rows, outputs, (part_gate, part_up, part_down))


def routed_body(inputs, grad_out, gates, expert_ids, slot_index, filter_taps, w_gate, w_up, w_down):
    tok_count, width = inputs.shape
    taps = filter_taps.shape[0]
    top_count = expert_ids.shape[1]
    experts = lax.axis_size("expert")
    capacity = tok_count * top_count // experts
    reach = taps - 1
    shift_count = (reach + tok_count - 1) // tok_count
    earlier = [from_behind(inputs, "seq", shift_by) for shift_by in range(shift_count, 0, -1)]
    extended = jnp.concatenate(earlier + [inputs], axis=0)[-(tok_count + reach) :]
    filtered = depthwise(extended, filter_taps[::-1]).astype(jnp.bfloat16)
    kept = slot_index < capacity
    dest = jnp.where(kept, expert_ids * capacity + slot_index, experts * capacity).reshape(-1)

    def place(values):
        rest = values.shape[1:]
        empty = jnp.zeros((experts * capacity,) + rest, values.dtype)
        return empty.at[dest].set(values, mode="drop").reshape((experts, capacity) + rest)

    def fetch(buffer):
        rest = buffer.shape[2:]
        flat = buffer.reshape((experts * capacity,) + rest)
        return jnp.take(flat, dest, axis=0, mode="fill", fill_value=0).reshape(
            (tok_count, top_count) + rest
        )

    token_send = place(
        jnp.broadcast_to(filtered[:, None, :], (tok_count, top_count, width)).reshape(-1, width)
    )
    gate_full, up_full, down_full = (
        lax.all_gather(w_gate, "seq", axis=1, tiled=True),
        lax.all_gather(w_up, "seq", axis=1, tiled=True),
        lax.all_gather(w_down, "seq", axis=1, tiled=True),
    )
    gate_mat = gate_full[0]
    up_mat = up_full[0]
    down_mat = down_full[0]
    scaled = (
        gates.astype(jnp.float32)[:, :, None] * grad_out.astype(jnp.float32)[:, None, :]
    ).astype(jnp.bfloat16)
    token_recv, scaled_recv = (
        lax.all_to_all(token_send, "expert", split_axis=0, concat_axis=0, tiled=True),
        lax.all_to_all(
            place(scaled.reshape(-1, width)), "expert", split_axis=0, concat_axis=0, tiled=True
        ),
    )
    grad_rows, outputs, partials = expert_pass(
        token_recv.reshape(-1, width), scaled_recv.reshape(-1, width), gate_mat, up_mat, down_mat
    )
    grad_back, output_back = (
        lax.all_to_all(
            grad_rows.reshape(experts, capacity, width),
            "expert",
            split_axis=0,
            concat_axis=0,
            tiled=True,
        ),
        lax.all_to_all(
            outputs.reshape(experts, capacity, width),
            "expert",
            split_axis=0,
            concat_axis=0,
            tiled=True,
        ),
    )
    output_rows = fetch(output_back)
    grad_gates = jnp.sum(
        grad_out.astype(jnp.float32)[:, None, :] * output_rows.astype(jnp.float32), axis=2
    ).astype(jnp.bfloat16)
    summed_gate, summed_up, summed_down = (
        lax.psum_scatter(
            partials[0][None].astype(jnp.bfloat16), "seq", scatter_dimension=1, tiled=True
        ).astype(jnp.float32),
        lax.psum_scatter(
            partials[1][None].astype(jnp.bfloat16), "seq", scatter_dimension=1, tiled=True
        ).astype(jnp.float32),
        lax.psum_scatter(
            partials[2][None].astype(jnp.bfloat16), "seq", scatter_dimension=1, tiled=True
        ).astype(jnp.float32),
    )
    grad_filtered = jnp.sum(fetch(grad_back).astype(jnp.float32), axis=1).astype(jnp.bfloat16)
    later = [from_behind(grad_filtered, "seq", -shift_by) for shift_by in range(1, shift_count + 1)]
    grad_extended = jnp.concatenate([grad_filtered] + later, axis=0)[: tok_count + reach]
    grad_inputs = depthwise(grad_extended, filter_taps).astype(jnp.bfloat16)
    local_taps = depthwise(extended, grad_filtered)[::-1]
    grad_filter = lax.psum(local_taps, ("expert", "seq"))
    return (
        grad_inputs,
        grad_gates,
        grad_filter,
        summed_gate.astype(jnp.bfloat16),
        summed_up.astype(jnp.bfloat16),
        summed_down.astype(jnp.bfloat16),
    )


def transforms(size):
    freq = 2.0 * np.pi * (np.arange(size // 2) + 0.5) / size
    angle = freq[:, None] * np.arange(size)[None, :]
    forward = np.concatenate([np.cos(angle), np.sin(angle)], axis=0)
    inverse = forward.T * (2.0 / size)

    def pieces(matrix):
        high = matrix.astype(jnp.bfloat16)
        low = (matrix - high.astype(np.float64)).astype(jnp.bfloat16)
        return high, low

    return pieces(forward) + pieces(inverse)


def mm(left, right):
    return jnp.dot(left, right, preferred_element_type=F32)


def dense_kernel(
    rows_ref, cot_ref, gates_ref, ids_ref, slots_ref, wg_ref, wu_ref, wd_ref, taps_ref,
    fh_ref, fl_ref, ih_ref, il_ref,
    gin_ref, gg_ref, gf_ref, dg_ref, du_ref, dd_ref,
    xext, tap_spec, x_spec, tall, gall, wall, hid, gpre, scaled, back, rall,
    part, sib_in, pair, cross_in, gext, gfs, gf_in, gfz, gfz_in, gfull,
    weigh, sums, sums_in,
    send_sem, recv_sem,
):
    z = lax.axis_index("expert")
    q = lax.axis_index("seq")
    tok, width = rows_ref.shape
    size = xext.shape[0]
    half = size // 2
    reach_at = size - tok
    dq = 2 * tok
    ff = hid.shape[1]
    fq = ff // 4
    chunk = 256
    chunks = width // chunk
    sib = q + 1 - 2 * (q % 2)
    cross = (q + 2) % 4
    far = (sib + 2) % 4

    def link(n, src, dst, axis, peer, arrival=None):
        return pltpu.make_async_remote_copy(
            src_ref=src, dst_ref=dst, send_sem=send_sem.at[n],
            recv_sem=recv_sem.at[n if arrival is None else arrival],
            device_id={axis: peer}, device_id_type=MESH,
        )

    def pick(a, b, c, d):
        return jnp.where(z == 0, a, jnp.where(z == 1, b, jnp.where(z == 2, c, d)))

    def hop(base, buf, origin, step):
        return link(
            base + (0 if step > 0 else 4) + origin, buf.at[origin], buf.at[origin],
            "expert", (z + 4 + step) % 4, base + origin,
        )

    def spread(base, buf, distance, send=True):
        for step in (1, -1):
            origin = z - step * distance
            has_origin = origin >= 0 if step > 0 else origin <= 3
            has_next = z < 3 if step > 0 else z > 0

            @pl.when(has_origin)
            def _(origin=origin, has_next=has_next, step=step):
                if distance and send:
                    hop(base, buf, origin, step).wait_recv()

                @pl.when(has_next)
                def _():
                    if send:
                        hop(base, buf, origin, step).start()
                    else:
                        hop(base, buf, origin, step).wait_send()

    barrier = pltpu.get_barrier_semaphore()
    for s in range(1, 4):
        pl.semaphore_signal(barrier, inc=1, device_id={"expert": (z + s) % 4}, device_id_type=MESH)
        pl.semaphore_signal(barrier, inc=1, device_id={"seq": (q + s) % 4}, device_id_type=MESH)

    ids = ids_ref[...]
    held = jnp.where(slots_ref[...] < tok, gates_ref[...].astype(F32), 0.0)
    eye = lax.broadcasted_iota(jnp.int32, (tok, tok), 0) == lax.broadcasted_iota(
        jnp.int32, (tok, tok), 1
    )

    def as_row(column):
        return jnp.sum(jnp.where(eye, column, 0.0), axis=0, keepdims=True)

    def as_column(row):
        return jnp.sum(jnp.where(eye, row, 0.0), axis=1, keepdims=True)

    weigh[z] = jnp.zeros(weigh.shape[1:], F32)
    for e in range(4):
        weigh[z, e:e + 1] = as_row(
            jnp.sum(jnp.where(ids == e, held, 0.0), axis=1, keepdims=True)
        )
    gall[z] = cot_ref[...]
    wall[q, :dq, :ff] = wg_ref[0]
    wall[q, :dq, ff:] = wu_ref[0]
    wall[q, dq:] = wd_ref[0]
    xext[pl.ds(reach_at, tok)] = rows_ref[...]
    pl.semaphore_wait(barrier, 6)

    halo = [
        link(n, rows_ref, xext.at[pl.ds(reach_at - (n + 1) * tok, tok)], "seq", (q + n + 1) % 4)
        for n in range(2)
    ]
    for n in range(2):
        @pl.when(q + n + 1 < 4)
        def _(n=n):
            halo[n].start()

        @pl.when(q < n + 1)
        def _(n=n):
            xext[pl.ds(reach_at - (n + 1) * tok, tok)] = jnp.zeros((tok, width), BF16)

    weighs = [
        link(30 + s, weigh.at[z], weigh.at[z], "expert", (z + s) % 4, 61 + z) for s in range(1, 4)
    ]
    for copy in weighs:
        copy.start()
    spread(37, gall, 0)
    w_sib = link(8, wall.at[q], wall.at[q], "seq", sib)
    w_cross = link(9, wall.at[q], wall.at[q], "seq", cross)
    w_sib.start()

    def cols(c):
        return pl.ds(pl.multiple_of(c * chunk, chunk), chunk)

    def forward(first, count, values):
        span = slice(first, first + count)
        return mm(fh_ref[:, span], values) + mm(fl_ref[:, span], values)

    def backward(first, count, spec):
        span = slice(first, first + count)
        high = spec.astype(BF16)
        low = (spec - high.astype(F32)).astype(BF16)
        return mm(ih_ref[span], high) + mm(il_ref[span], high) + mm(ih_ref[span], low)

    taps = taps_ref.shape[0]

    @pl.loop(0, chunks)
    def _(c):
        tap_spec[:, cols(c)] = forward(0, taps, taps_ref[:, cols(c)])

    spread(37, gall, 1)
    for n in range(2):
        @pl.when(q >= n + 1)
        def _(n=n):
            halo[n].wait_recv()

    w_cross.start()

    @pl.loop(0, chunks)
    def _(c):
        spec = forward(0, size, xext[:, cols(c)])
        x_spec[:, cols(c)] = spec
        xc, xs = spec[:half], spec[half:]
        hc, hs = tap_spec[:half, cols(c)], tap_spec[half:, cols(c)]
        prod = jnp.concatenate([xc * hc - xs * hs, xc * hs + xs * hc], axis=0)
        tall[z, :, cols(c)] = backward(reach_at, tok, prod).astype(BF16)

    spread(45, tall, 0)
    spread(37, gall, 2)
    spread(45, tall, 1)

    w_cross.wait_recv()
    w_far = link(10, wall.at[cross], wall.at[cross], "seq", sib)
    w_far.start()
    w_sib.wait_recv()
    w_far.wait_recv()

    def turned(left, right):
        return lax.dot_general(left, right, (((1,), (1,)), ((), ())), preferred_element_type=F32)

    origins = [z, pick(1, 0, 1, 2), pick(2, 2, 3, 1), pick(3, 3, 0, 0)]
    sublanes = lax.broadcasted_iota(jnp.int32, weigh.shape[1:], 0)
    gate_sums = [
        link(33 + s, sums.at[s], sums_in.at[z], "expert", origins[s], 57 + z)
        for s in range(1, 4)
    ]
    backs = [
        link(10 + s, back.at[s], rall.at[z], "expert", origins[s], 53 + z) for s in range(1, 4)
    ]
    for s in range(4):
        origin = origins[s]
        if s == 1:
            spread(37, gall, 3)
            for k in range(1, 4):
                peer = (z + k) % 4
                link(30 + k, weigh.at[peer], weigh.at[peer], "expert", peer, 61 + peer).wait_recv()
        elif s > 1:
            spread(45, tall, s)
        span = pl.ds(s * tok, tok)
        pre = mm(tall[origin, :, 0:dq], wall[0, :dq, :])
        for k in range(1, 4):
            pre += mm(tall[origin, :, k * dq:(k + 1) * dq], wall[k, :dq, :])
        cot = gall[origin]
        weight = as_column(
            jnp.sum(jnp.where(sublanes == z, weigh[origin], 0.0), axis=0, keepdims=True)
        )
        raw = jnp.concatenate([turned(cot, wall[k, dq:, :]) for k in range(4)], axis=1)
        gate, up = pre[:, :ff], pre[:, ff:]
        sigma = jax.nn.sigmoid(gate)
        swish = gate * sigma
        hidden = (swish * up).astype(BF16)
        gg = jnp.sum(hidden.astype(F32) * raw, axis=1, keepdims=True)
        grad_hidden = raw * weight
        grad_gate = grad_hidden * up * (sigma * (1.0 + gate * (1.0 - sigma)))
        gp = jnp.concatenate([grad_gate.astype(BF16), (grad_hidden * swish).astype(BF16)], axis=1)
        hid[span] = hidden
        gpre[span] = gp
        scaled[span] = (weight * cot.astype(F32)).astype(BF16)
        target, at = (back, s) if s else (rall, z)
        for k in range(4):
            target[at, :, k * dq:(k + 1) * dq] = turned(gp, wall[k, :dq, :]).astype(BF16)
        (sums if s else sums_in)[at] = jnp.broadcast_to(as_row(gg), sums.shape[1:])
        if s:
            gate_sums[s - 1].start()
            backs[s - 1].start()

    def across(left, right):
        return lax.dot_general(left, right, (((0,), (0,)), ((), ())), preferred_element_type=F32)

    def partial(slot, dest):
        top = jnp.zeros((dq, 2 * ff), F32)
        low = jnp.zeros((fq, width), F32)
        wide = pl.ds(pl.multiple_of(dest * dq, dq), dq)
        thin = pl.ds(pl.multiple_of(dest * fq, fq), fq)
        for s in range(4):
            top += across(tall[origins[s], :, wide], gpre[pl.ds(s * tok, tok)])
        low = across(hid[:, thin], scaled[...])
        part[slot, :dq] = top.astype(BF16)
        part[slot, dq:] = low.astype(BF16)

    to_sib = [link(14 + n, part.at[n], sib_in.at[n], "seq", sib) for n in range(2)]
    partial(0, far)
    to_sib[0].start()
    partial(1, sib)
    to_sib[1].start()
    partial(2, cross)
    to_sib[0].wait_recv()
    pair[...] = (part[2].astype(F32) + sib_in[0].astype(F32)).astype(BF16)
    to_cross = link(16, pair, cross_in, "seq", cross)
    to_cross.start()
    partial(3, q)

    for s in range(1, 4):
        peer = (z + s) % 4
        link(10 + s, back.at[s], rall.at[peer], "expert", peer, 53 + peer).wait_recv()
    total = jnp.zeros((tok, width), F32)
    for s in range(4):
        total += rall[s].astype(F32)
    gext[pl.ds(0, tok)] = total.astype(BF16)
    halo_back = [
        link(17 + n, gext.at[pl.ds(0, tok)], gext.at[pl.ds((n + 1) * tok, tok)], "seq", (q + 3 - n) % 4)
        for n in range(2)
    ]
    for n in range(2):
        @pl.when(q >= n + 1)
        def _(n=n):
            halo_back[n].start()

        @pl.when(q + n + 1 >= 4)
        def _(n=n):
            gext[pl.ds((n + 1) * tok, tok)] = jnp.zeros((tok, width), BF16)

    for s in range(1, 4):
        peer = (z + s) % 4
        link(33 + s, sums.at[s], sums_in.at[peer], "expert", peer, 57 + peer).wait_recv()
    gate_grads = jnp.zeros(ids.shape, F32)
    for s in range(4):
        gate_grads += jnp.where(ids == s, as_column(sums_in[s, 0:1]), 0.0)
    gg_ref[...] = jnp.where(slots_ref[...] < tok, gate_grads, 0.0).astype(BF16)

    quarter = taps // 4

    @pl.loop(0, chunks)
    def _(c):
        spec = forward(reach_at, tok, gext[pl.ds(0, tok), cols(c)])
        gc, gs = spec[:half], spec[half:]
        xc, xs = x_spec[:half, cols(c)], x_spec[half:, cols(c)]
        prod = jnp.concatenate([gc * xc + gs * xs, gs * xc - gc * xs], axis=0)
        result = backward(0, taps, prod).astype(BF16)
        for k in range(4):
            gfs[k, :, cols(c)] = result[k * quarter:(k + 1) * quarter]

    gf_seq = [
        link(18 + s, gfs.at[(q + s) % 4], gf_in.at[s], "seq", (q + s) % 4) for s in range(1, 4)
    ]
    for copy in gf_seq:
        copy.start()

    for copy in gf_seq:
        copy.wait_recv()
    mine = gfs[q].astype(F32)
    for s in range(1, 4):
        mine += gf_in[s].astype(F32)
    piece = quarter // 4
    for k in range(4):
        gfz[k] = mine[k * piece:(k + 1) * piece].astype(BF16)
    gf_exp = [
        link(21 + s, gfz.at[(z + s) % 4], gfz_in.at[s], "expert", (z + s) % 4) for s in range(1, 4)
    ]
    for copy in gf_exp:
        copy.start()

    for n in range(2):
        @pl.when(q + n + 1 < 4)
        def _(n=n):
            halo_back[n].wait_recv()

    for copy in gf_exp:
        copy.wait_recv()
    mine = gfz[z].astype(F32)
    for s in range(1, 4):
        mine += gfz_in[s].astype(F32)
    gfull[q, z] = mine.astype(BF16)
    gf_out = [
        link(24 + s, gfull.at[q, z], gfull.at[q, z], "expert", (z + s) % 4) for s in range(1, 4)
    ]
    for copy in gf_out:
        copy.start()

    @pl.loop(0, chunks)
    def _(c):
        spec = forward(0, size, gext[:, cols(c)])
        gc, gs = spec[:half], spec[half:]
        hc, hs = tap_spec[:half, cols(c)], tap_spec[half:, cols(c)]
        prod = jnp.concatenate([gc * hc + gs * hs, gs * hc - gc * hs], axis=0)
        gin_ref[:, cols(c)] = backward(0, tok, prod).astype(BF16)

    for copy in gf_out:
        copy.wait_recv()
    gf_last = [link(27 + s, gfull.at[q], gfull.at[q], "seq", (q + s) % 4) for s in range(1, 4)]
    for copy in gf_last:
        copy.start()

    to_sib[1].wait_recv()
    to_cross.wait_recv()
    weights = (
        part[3].astype(F32) + sib_in[1].astype(F32) + cross_in[...].astype(F32)
    ).astype(BF16)
    dg_ref[0] = weights[:dq, :ff]
    du_ref[0] = weights[:dq, ff:]
    dd_ref[0] = weights[dq:]

    for copy in gf_last:
        copy.wait_recv()
    for a in range(4):
        for b in range(4):
            gf_ref[pl.ds((a * 4 + b) * piece, piece)] = gfull[a, b]

    for n in range(2):
        @pl.when(q + n + 1 < 4)
        def _(n=n):
            halo[n].wait_send()

        @pl.when(q >= n + 1)
        def _(n=n):
            halo_back[n].wait_send()
    for d in range(3):
        spread(37, gall, d, False)
        spread(45, tall, d, False)
    for copy in (
        weighs + gate_sums + [w_sib, w_cross, w_far] + backs + to_sib + [to_cross]
        + gf_seq + gf_exp + gf_out + gf_last
    ):
        copy.wait_send()


def dense_body(inputs, grad_out, gates, expert_ids, slot_index, filter_taps, w_gate, w_up, w_down):
    tok, width = inputs.shape
    taps = filter_taps.shape[0]
    ff = w_gate.shape[2]
    size = taps + tok
    rows = w_gate.shape[1] + w_down.shape[1]
    vm = lambda *shape: pltpu.VMEM(shape, BF16)
    outs = pl.pallas_call(
        dense_kernel,
        out_shape=(
            jax.ShapeDtypeStruct((tok, width), BF16),
            jax.ShapeDtypeStruct(gates.shape, BF16),
            jax.ShapeDtypeStruct((taps, width), BF16),
            jax.ShapeDtypeStruct(w_gate.shape, BF16),
            jax.ShapeDtypeStruct(w_up.shape, BF16),
            jax.ShapeDtypeStruct(w_down.shape, BF16),
        ),
        in_specs=[pl.BlockSpec(memory_space=pltpu.VMEM)] * 13,
        out_specs=(pl.BlockSpec(memory_space=pltpu.VMEM),) * 6,
        scratch_shapes=[
            vm(size, width), pltpu.VMEM((size, width), F32), pltpu.VMEM((size, width), F32),
            vm(4, tok, width), vm(4, tok, width), vm(4, rows, width),
            vm(4 * tok, ff), vm(4 * tok, 2 * ff), vm(4 * tok, width),
            vm(4, tok, width), vm(4, tok, width),
            vm(4, rows, width), vm(2, rows, width), vm(rows, width), vm(rows, width),
            vm(size, width), vm(4, taps // 4, width), vm(4, taps // 4, width),
            vm(4, taps // 16, width), vm(4, taps // 16, width),
            vm(4, 4, taps // 16, width),
            pltpu.VMEM((4, 8, tok), F32), pltpu.VMEM((4, 8, tok), F32), pltpu.VMEM((4, 8, tok), F32),
            pltpu.SemaphoreType.DMA((65,)), pltpu.SemaphoreType.DMA((65,)),
        ],
        compiler_params=pltpu.CompilerParams(
            collective_id=0, has_side_effects=True, vmem_limit_bytes=52 * 1024 * 1024
        ),
    )(
        inputs, grad_out, gates, expert_ids, slot_index, w_gate, w_up, w_down, filter_taps,
        *[jnp.asarray(m) for m in transforms(size)],
    )
    return outs[:2] + (outs[2].astype(F32),) + outs[3:]


def body_of(mesh):
    def body(*args):
        top_count = args[3].shape[1]
        tok, taps, dq = args[0].shape[0], args[5].shape[0], args[6].shape[1]
        small = mesh.shape["expert"] == top_count == 4 and mesh.shape["seq"] == 4
        if small and tok == 128 and taps == 2 * tok and dq == 2 * tok and 2 * args[6].shape[2] == args[0].shape[1]:
            return dense_body(*args)
        return routed_body(*args)

    return body


def solution(mesh):
    return jax.shard_map(
        body_of(mesh),
        mesh=mesh,
        in_specs=(
            P(("groups", "expert", "seq"), None),
            P(("groups", "expert", "seq"), None),
            P(("groups", "expert", "seq"), None),
            P(("groups", "expert", "seq"), None),
            P(("groups", "expert", "seq"), None),
            P(),
            P("expert", "seq", None),
            P("expert", "seq", None),
            P("expert", "seq", None),
        ),
        out_specs=(
            P(("groups", "expert", "seq"), None),
            P(("groups", "expert", "seq"), None),
            P("groups", None),
            P(("groups", "expert"), "seq", None),
            P(("groups", "expert"), "seq", None),
            P(("groups", "expert"), "seq", None),
        ),
        check_vma=False,
    )
```
